512 devices in a mesh: seq: 64 (over z, y), head: 8 (over x, core).
Axes of the slice: x: 4, y: 4, z: 16, core: 2. Of those that a mesh axis runs over, the one named last changes fastest.
Arguments:
- tokens: bfloat16 [32768, 1024], P('seq', 'head'), may hold values from -6 to 6
- w_qkv: bfloat16 [1, 1024, 3, 1024], P(None, None, None, 'head'), may hold values from -0.1875 to 0.1875
- w_out: bfloat16 [1, 1024, 1024], P(None, 'head'), may hold values from -0.1875 to 0.1875
- gain_in: bfloat16 [1, 1024], replicated, may hold values from 0.099609375 to 1.8984375
- gain_mid: bfloat16 [1, 1024], P(None, 'head'), may hold values from 0.099609375 to 1.8984375
Outputs:
- hidden: bfloat16 [32768, 1024], P('seq', 'head')
The draws below stay inside these ranges and needn't reach their ends.
All inputs are finite; a program needn't handle non-finite values.
Results may differ from the reference program's by a relative error of at most 0.014.
Values may be sent and summed in bfloat16 or wider, within the bound.
No kernel may reach another device: no remote copies, remote signals or barrier semaphores. Data moves between devices by JAX's collectives and lax.ppermute only.
A program may use at most 128 MiB of HBM per device.

```python
import math
import jax
import jax.numpy as jnp
from jax import lax

D = 1024
H = 16
DH = 64
LAYERS = 1
TOK_DEV = 512
FEAT = 2080
TOKENS = 32768
N_SEQ = 64


def block_levels(stream_key, extent, shards, low, largest):
    def one(axis_at, parts):
        heights = jax.random.uniform(jax.random.fold_in(jax.random.fold_in(stream_key, 6), axis_at), (parts,), jnp.float32, low / len(shards), largest / len(shards))
        return jnp.repeat(jnp.exp(heights), extent[axis_at] // parts).reshape((-1,) + (1,) * (len(extent) - axis_at - 1))

    level = one(*shards[0])
    for cut in shards[1:]:
        level = level * one(*cut)
    return level


def gaussian(key, shape, scale, most, cuts=(), kind=jnp.bfloat16):
    level = block_levels(key, shape, cuts, -0.22, 0.18) if cuts else 1.0
    entries = jax.random.normal(key, shape, jnp.float32) * scale * level
    return jnp.minimum(jnp.maximum(entries, -most), most).astype(kind)


def setup_inputs(seed: int = 0) -> dict:
    splits = jax.random.split(jax.random.key(seed), 6)
    return {
        "tokens": gaussian(splits[0], (TOKENS, D), 1.0, 6.0, ((0, 64), (1, 8))),
        "w_qkv": gaussian(splits[1], (LAYERS, D, 3, H * DH), D ** -0.5, 0.1875, ((3, 8),)),
        "w_out": gaussian(splits[2], (LAYERS, H * DH, D), (H * DH) ** -0.5, 0.1875, ((1, 8),)),
        "gain_in": jnp.clip(1.0 + 0.18 * jax.random.normal(splits[3], (LAYERS, D), jnp.float32), 0.099609375, 1.8984375).astype(jnp.bfloat16),
        "gain_mid": jnp.clip(1.0 + 0.18 * jax.random.normal(splits[4], (LAYERS, H * DH), jnp.float32), 0.099609375, 1.8984375).astype(jnp.bfloat16),
    }


EPSILON = 1e-06
SQRT_TWO = math.sqrt(2.0)

def expand(columns):
    pieces = []
    for column in range(columns.shape[1]):
        leading = columns[:, column:column + 1, :]
        pieces.append(leading * leading)
        pieces.append(SQRT_TWO * leading * columns[:, column + 1:, :])
    return jnp.concatenate(pieces, axis=1)

def highest_einsum(form, left, right):
    return jnp.einsum(form, left.astype(jnp.float32), right.astype(jnp.float32), precision=lax.Precision.HIGHEST)

def run_layer(hidden, weight_qkv, weight_out, gain_first, gain_second):
    blocks = hidden.reshape(N_SEQ, TOK_DEV, D)
    weight_heads = weight_qkv.reshape(D, 3, H, DH)
    row_ids = jnp.arange(TOK_DEV, dtype=jnp.int32)
    causal = row_ids[:, None] >= row_ids[None, :]

    def one_block(carry, block):
        prefix_state, prefix_norm = carry
        wide = block.astype(jnp.float32)
        normed = (wide * lax.rsqrt(lax.optimization_barrier(jnp.mean(wide * wide, axis=1, keepdims=True)) + EPSILON) * gain_first.astype(jnp.float32)).astype(jnp.bfloat16)
        projected = highest_einsum('td,dche->chet', normed, weight_heads).astype(jnp.bfloat16)
        query_cols, key_cols, value_cols = (projected[0], projected[1], projected[2])
        key_feats = expand(key_cols.astype(jnp.float32)).astype(jnp.bfloat16)
        query_feats = (expand(query_cols.astype(jnp.float32)) / DH).astype(jnp.bfloat16)
        scores = highest_einsum('hdt,hds->hts', query_cols, key_cols)
        weights = jnp.where(causal[None], scores * scores / DH, 0.0)
        local_den = lax.optimization_barrier(jnp.sum(weights, axis=2))
        local_num = highest_einsum('hts,hes->the', weights.astype(jnp.bfloat16), value_cols)
        num_prefix = highest_einsum('hft,hfe->the', query_feats, prefix_state.astype(jnp.bfloat16))
        den_prefix = highest_einsum('hft,hf->th', query_feats, prefix_norm.astype(jnp.bfloat16))
        attended = (local_num + num_prefix) / (1.0 + local_den.T + den_prefix)[:, :, None]
        attended = attended.reshape(TOK_DEV, H * DH)
        inverse_rms = lax.rsqrt(lax.optimization_barrier(jnp.mean(attended * attended, axis=1, keepdims=True)) + EPSILON)
        mixed_in = (attended * inverse_rms * gain_second.astype(jnp.float32)).astype(jnp.bfloat16)
        update = jnp.dot(mixed_in, weight_out, preferred_element_type=jnp.float32)
        new_block = (wide + update).astype(jnp.bfloat16)
        block_state = highest_einsum('hft,het->hfe', key_feats, value_cols)
        block_norm = lax.optimization_barrier(jnp.sum(key_feats.astype(jnp.float32), axis=2))
        return ((prefix_state + block_state, prefix_norm + block_norm), new_block)
    initial = (jnp.zeros((H, FEAT, DH), jnp.float32), jnp.zeros((H, FEAT), jnp.float32))
    final_carry, new_blocks = lax.scan(one_block, initial, blocks)
    return new_blocks.reshape(TOKENS, D)

def reference(tokens, w_qkv, w_out, gain_in, gain_mid):
    hidden = tokens
    for layer_index in range(LAYERS):
        hidden = run_layer(hidden, w_qkv[layer_index], w_out[layer_index], gain_in[layer_index], gain_mid[layer_index])
    return hidden
```

```python
import jax
import jax.numpy as jnp
from jax import lax
from jax.experimental import pallas as pl
from jax.experimental.pallas import tpu as pltpu
from jax.sharding import PartitionSpec as P

D = 1024
H = 16
DH = 64
T = 512
EPSILON = 1e-06
SHIFTS = 32
PLANE = 4
PLANES = 16
SLICE = 544
PIECE = 40
F32 = jnp.float32
BF16 = jnp.bfloat16
VMEM = pl.BlockSpec(memory_space=pltpu.VMEM)
SMEM = pl.BlockSpec(memory_space=pltpu.SMEM)
X_GROUPS = [[0, 2, 4, 6], [1, 3, 5, 7]]
Y_GROUPS = [[PLANE * z + y for y in range(PLANE)] for z in range(PLANES)]
Z_GROUPS = [[PLANE * z + y for z in range(PLANES)] for y in range(PLANE)]
CORE_SWAP = [(h, h ^ 1) for h in range(8)]


def dot(a, b):
    return jnp.dot(a, b, preferred_element_type=F32)


def call(kernel, outs, scratch=(), flops=0, moved=0, **kw):
    return pl.pallas_call(
        kernel,
        out_shape=outs,
        scratch_shapes=list(scratch),
        cost_estimate=pl.CostEstimate(flops=flops, bytes_accessed=moved, transcendentals=0),
        compiler_params=pltpu.CompilerParams(vmem_limit_bytes=40 * 1024 * 1024),
        **kw,
    )


def feature_rows(wide):
    base = wide.astype(BF16)
    for low in range(16):
        turned = (pltpu.roll(wide, DH - low, 0) if low else wide).astype(BF16)
        for high in range(3):
            shift = 16 * high + low
            if shift > SHIFTS:
                continue
            moved = turned
            if high:
                moved = jnp.concatenate([turned[16 * high :], turned[: 16 * high]], axis=0)
            yield shift, base * moved


def project_kernel(core, own, other, gain, weights, sent, q_t, k_nat, v_t, k_t, v_diag):
    c = core[0]
    for chunk in range(4):
        rows = pl.ds(128 * chunk, 128)
        total = jnp.zeros((128, 1), F32)
        for x in range(4):
            for part in (own, other):
                wide = part[x, rows, :].astype(F32)
                total += jnp.sum(wide * wide, axis=1, keepdims=True)
        inverse = lax.rsqrt(total / D + EPSILON)
        projected = jnp.zeros((128, 384), F32)
        for x in range(4):
            first, second = 2 * x + c, 2 * x + 1 - c
            left = (own[x, rows, :].astype(F32) * inverse * gain[pl.ds(first, 1), :]).astype(BF16)
            right = (other[x, rows, :].astype(F32) * inverse * gain[pl.ds(second, 1), :]).astype(BF16)
            both = jnp.concatenate(
                [
                    jnp.concatenate([weights[kind, block] for kind in range(3)], axis=1)
                    for block in (first, second)
                ],
                axis=0,
            )
            projected += dot(jnp.concatenate([left, right], axis=1), both)
        rounded = projected.astype(BF16)
        k_nat[rows, :] = rounded[:, 128:256]
        values = rounded[:, 256:384]
        lane = lax.broadcasted_iota(jnp.int32, values.shape, 1)
        v_diag[rows, :] = jnp.where(lane < DH, values, jnp.zeros_like(values))
        v_diag[pl.ds(T + 128 * chunk, 128), :] = jnp.where(lane >= DH, values, jnp.zeros_like(values))
        turned = rounded.astype(F32).T
        q_t[:, rows] = turned[0:128].astype(BF16)
        k_t[:, rows] = turned[128:256]
        v_t[:, rows] = turned[256:384].astype(BF16)
    right = v_diag[...]
    for (shift, first), (_, second) in zip(feature_rows(k_t[0:DH, :]), feature_rows(k_t[DH:, :])):
        state = dot(jnp.concatenate([first, second], axis=1), right).astype(BF16)
        if shift == SHIFTS:
            for y in range(PLANE):
                sent[y, 512:528, :] = state[16 * y : 16 * (y + 1)]
        else:
            sent[shift // 8, DH * (shift % 8) : DH * (shift % 8 + 1), :] = state
    gram = dot(k_t[...].astype(BF16), k_nat[...])
    lane = lax.broadcasted_iota(jnp.int32, (DH, 128), 1)
    gram = jnp.where(lane < DH, gram[0:DH], gram[DH:]).astype(BF16)
    for y in range(PLANE):
        sent[y, 528:544, :] = gram[16 * y : 16 * (y + 1)]


def merge_kernel(blocks, total):
    def summed(start, size):
        rows = slice(start, start + size)
        pairs = [blocks[y, rows, :].astype(F32) for y in range(PLANE)]
        return (pairs[0] + pairs[1]) + (pairs[2] + pairs[3])

    for z in range(PLANES):
        total[z, 0:32, :] = summed(32 * z, 32).astype(BF16)
    last, gram = summed(512, 16), summed(528, 16)
    row = lax.broadcasted_iota(jnp.int32, (PLANES, 8, 128), 1)
    extra = jnp.where(row == 0, last[:, None, :], jnp.where(row == 1, gram[:, None, :], 0.0))
    total[:, 32:40, :] = extra.astype(BF16)


def prefix_kernel(blocks, prefix):
    running = jnp.zeros((PIECE, 128), F32)
    for z in range(PLANES):
        prefix[z] = running.astype(BF16)
        if z < PLANES - 1:
            running += blocks[z].astype(F32)


def spread_kernel(prefix, blocks, out):
    def spread(running, start, size):
        rows = slice(start, start + size)
        for y in range(PLANE):
            out[y, rows, :] = running.astype(BF16)
            if y < PLANE - 1:
                running += blocks[y, rows, :].astype(F32)

    for z in range(PLANES):
        spread(prefix[z, 0:32, :].astype(F32), 32 * z, 32)
    extra = prefix[:, 32:40, :].astype(F32)
    spread(extra[:, 0, :], 512, 16)
    spread(extra[:, 1, :], 528, 16)


def local_kernel(q_t, k_nat, v_t, num, den):
    queries = q_t[...]
    row = lax.broadcasted_iota(jnp.int32, queries.shape, 0)
    for h in range(2):
        masked = jnp.where((row >= DH * h) & (row < DH * (h + 1)), queries, jnp.zeros_like(queries))
        for j in range(2):
            cols = slice(256 * j, 256 * (j + 1))
            total = jnp.zeros((DH, 256), F32)
            weight_sum = jnp.zeros((1, 256), F32)
            for i in range(j + 1):
                scores = dot(k_nat[256 * i : 256 * (i + 1), :], masked[:, cols])
                weights = scores * scores * (1.0 / DH)
                if i == j:
                    s_ids = lax.broadcasted_iota(jnp.int32, weights.shape, 0)
                    t_ids = lax.broadcasted_iota(jnp.int32, weights.shape, 1)
                    weights = jnp.where(s_ids <= t_ids, weights, 0.0)
                weight_sum += jnp.sum(weights, axis=0, keepdims=True)
                values = v_t[DH * h : DH * (h + 1), 256 * i : 256 * (i + 1)]
                total += dot(values, weights.astype(BF16))
            num[DH * h : DH * (h + 1), cols] = total
            den[h : h + 1, cols] = weight_sum
    den[2:8, :] = jnp.zeros((6, T), F32)


def finish_kernel(core, prefix, num, den, q_t, gain, weights, keep, give, feats):
    c = core[0]
    gram = jnp.concatenate([prefix[y, 528:544, :] for y in range(PLANE)], axis=0).astype(F32).T
    gram = gram.astype(BF16)
    dens = []
    for h in range(2):
        queries = q_t[DH * h : DH * (h + 1), :]
        wide = queries.astype(F32)
        both = dot(gram[DH * h : DH * (h + 1), :], queries)
        dens.append(jnp.sum(both * wide, axis=0, keepdims=True) * (1.0 / DH))
        for shift, product in feature_rows(wide):
            scale = (1.0 if shift in (0, SHIFTS) else 2.0) / DH
            feats[h, DH * shift : DH * (shift + 1), :] = product * jnp.asarray(scale, BF16)
    sums = [num[0:DH, :], num[DH:, :]]
    for group in range(9):
        if group < 8:
            state = prefix[group // 2, 256 * (group % 2) : 256 * (group % 2 + 1), :]
        else:
            state = jnp.concatenate([prefix[y, 512:528, :] for y in range(PLANE)], axis=0)
        turned = state.astype(F32).T.astype(BF16)
        rows = pl.ds(256 * group, 256 if group < 8 else DH)
        for h in range(2):
            sums[h] += dot(turned[DH * h : DH * (h + 1), :], feats[h, rows, :])
    attended = jnp.concatenate(
        [sums[h] / (1.0 + den[h : h + 1, :] + dens[h]) for h in range(2)], axis=0
    )
    squares = jnp.sum(attended * attended, axis=0, keepdims=True)
    column = jnp.broadcast_to(gain[...].astype(F32), (128, 128)).T
    mixed = jnp.concatenate(
        [attended[:, 128 * i : 128 * (i + 1)] * column for i in range(4)], axis=1
    ).astype(BF16)
    extra = split_rows(squares)
    for x in range(4):
        keep[x, 0:128, :] = dot(weights[2 * x + c], mixed).astype(BF16)
        give[x, 0:128, :] = dot(weights[2 * x + 1 - c], mixed).astype(BF16)
        keep[x, 128:136, :] = extra
        give[x, 128:136, :] = extra


def split_rows(squares):
    high = squares.astype(BF16).astype(F32)
    row = lax.broadcasted_iota(jnp.int32, (8, T), 0)
    return jnp.where(row == 0, high, jnp.where(row == 1, squares - high, 0.0)).astype(BF16)


def pair_kernel(keep, received, out):
    for x in range(4):
        out[x, 0:128, :] = (keep[x, 0:128, :].astype(F32) + received[x, 0:128, :].astype(F32)).astype(BF16)
        extra = keep[x, 128:136, :].astype(F32) + received[x, 128:136, :].astype(F32)
        out[x, 128:136, :] = split_rows(jnp.sum(extra, axis=0, keepdims=True))


def output_kernel(parts, hidden, out):
    total = parts[0, 0:128, :].astype(F32)
    extra = parts[0, 128:136, :].astype(F32)
    for x in range(1, 4):
        total += parts[x, 0:128, :].astype(F32)
        extra += parts[x, 128:136, :].astype(F32)
    squares = jnp.sum(extra, axis=0, keepdims=True)
    update = total * lax.rsqrt(squares / D + EPSILON)
    out[...] = (hidden[...].astype(F32) + update.T).astype(BF16)


def exchange(blocks, axis, groups):
    return lax.all_to_all(blocks, axis, 0, 0, axis_index_groups=groups)


def shards(tokens, w_qkv, w_out, gain_in, gain_mid):
    core = (lax.axis_index("head") & 1).astype(jnp.int32)[None]
    shape = jax.ShapeDtypeStruct
    weights = w_qkv[0].transpose(1, 0, 2).reshape(3, 8, 128, 128)
    gains = gain_in.reshape(8, 128).astype(F32)
    out_weights = w_out[0].reshape(128, 8, 128).transpose(1, 2, 0)
    own = exchange(jnp.broadcast_to(tokens, (4, T, 128)), "head", X_GROUPS)
    other = lax.ppermute(own, "head", CORE_SWAP)
    sent, q_t, k_nat, v_t = call(
        project_kernel,
        (
            shape((PLANE, SLICE, 128), BF16),
            shape((128, T), BF16),
            shape((T, 128), BF16),
            shape((128, T), BF16),
        ),
        scratch=[pltpu.VMEM((128, T), F32), pltpu.VMEM((2 * T, 128), BF16)],
        flops=2 * T * D * 384 + 2 * 2112 * T * 256,
        moved=3000000,
        in_specs=[SMEM, VMEM, VMEM, VMEM, VMEM],
        out_specs=(VMEM,) * 4,
    )(core, own, other, gains, weights)
    blocks = exchange(sent, "seq", Y_GROUPS)
    num, den = call(
        local_kernel,
        (shape((128, T), F32), shape((8, T), F32)),
        flops=2 * 2 * T * T * 128,
        moved=1000000,
        in_specs=[VMEM] * 3,
        out_specs=(VMEM,) * 2,
    )(q_t, k_nat, v_t)
    pieces = shape((PLANES, PIECE, 128), BF16)
    total = call(merge_kernel, pieces, moved=800000, in_specs=[VMEM], out_specs=VMEM)(blocks)
    received = exchange(total, "seq", Z_GROUPS)
    prefix = call(prefix_kernel, pieces, moved=400000, in_specs=[VMEM], out_specs=VMEM)(received)
    prefix = exchange(prefix, "seq", Z_GROUPS)
    spread = call(
        spread_kernel,
        shape((PLANE, SLICE, 128), BF16),
        moved=1300000,
        in_specs=[VMEM] * 2,
        out_specs=VMEM,
    )(prefix, blocks)
    spread = exchange(spread, "seq", Y_GROUPS)
    partial = shape((4, 136, T), BF16)
    keep, give = call(
        finish_kernel,
        (partial, partial),
        scratch=[pltpu.VMEM((2, 2112, T), BF16)],
        flops=2 * 2112 * T * 128,
        moved=2500000,
        in_specs=[SMEM] + [VMEM] * 6,
        out_specs=(VMEM,) * 2,
    )(core, spread, num, den, q_t, gain_mid, out_weights)
    received = lax.ppermute(give, "head", CORE_SWAP)
    paired = call(pair_kernel, partial, moved=1600000, in_specs=[VMEM] * 2, out_specs=VMEM)(
        keep, received
    )
    parts = exchange(paired, "head", X_GROUPS)
    return call(
        output_kernel,
        shape((T, 128), BF16),
        moved=900000,
        in_specs=[VMEM] * 2,
        out_specs=VMEM,
    )(parts, tokens)


def solution(mesh):
    placed = (
        P("seq", "head"),
        P(None, None, None, "head"),
        P(None, "head", None),
        P(),
        P(None, "head"),
    )
    return jax.shard_map(
        shards, mesh=mesh, in_specs=placed, out_specs=P("seq", "head"), check_vma=False
    )
```

```python
import jax
import jax.numpy as jnp
from jax import lax
from jax.experimental import pallas as pl
from jax.experimental.pallas import tpu as pltpu
from jax.sharding import PartitionSpec as P

D = 1024
H = 16
DH = 64
T = 512
EPSILON = 1e-06
SHIFTS = 32
PLANE = 8
PLANES = 8
MAIN = 2048 // PLANE
EDGE = DH // PLANE
SLICE = MAIN + 2 * EDGE
PIECE = 40
F32 = jnp.float32
BF16 = jnp.bfloat16
VMEM = pl.BlockSpec(memory_space=pltpu.VMEM)
SMEM = pl.BlockSpec(memory_space=pltpu.SMEM)
X_GROUPS = [[0, 2, 4, 6], [1, 3, 5, 7]]
NEAR_GROUPS = [[PLANE * z + y for y in range(PLANE)] for z in range(PLANES)]
FAR_GROUPS = [[PLANE * z + y for z in range(PLANES)] for y in range(PLANE)]
CORE_SWAP = [(h, h ^ 1) for h in range(8)]


def dot(a, b):
    return jnp.dot(a, b, preferred_element_type=F32)


def call(kernel, outs, scratch=(), flops=0, moved=0, **kw):
    return pl.pallas_call(
        kernel,
        out_shape=outs,
        scratch_shapes=list(scratch),
        cost_estimate=pl.CostEstimate(flops=flops, bytes_accessed=moved, transcendentals=0),
        compiler_params=pltpu.CompilerParams(vmem_limit_bytes=40 * 1024 * 1024),
        **kw,
    )


def feature_rows(wide):
    base = wide.astype(BF16)
    for low in range(16):
        turned = (pltpu.roll(wide, DH - low, 0) if low else wide).astype(BF16)
        for high in range(3):
            shift = 16 * high + low
            if shift > SHIFTS:
                continue
            moved = turned
            if high:
                moved = jnp.concatenate([turned[16 * high :], turned[: 16 * high]], axis=0)
            yield shift, base * moved


def project_kernel(core, own, other, gain, weights, sent, q_t, k_nat, v_t, k_t, v_diag):
    c = core[0]
    for chunk in range(4):
        rows = pl.ds(128 * chunk, 128)
        total = jnp.zeros((128, 1), F32)
        for x in range(4):
            for part in (own, other):
                wide = part[x, rows, :].astype(F32)
                total += jnp.sum(wide * wide, axis=1, keepdims=True)
        inverse = lax.rsqrt(total / D + EPSILON)
        projected = jnp.zeros((128, 384), F32)
        for x in range(4):
            first, second = 2 * x + c, 2 * x + 1 - c
            left = (own[x, rows, :].astype(F32) * inverse * gain[pl.ds(first, 1), :]).astype(BF16)
            right = (other[x, rows, :].astype(F32) * inverse * gain[pl.ds(second, 1), :]).astype(BF16)
            both = jnp.concatenate(
                [
                    jnp.concatenate([weights[kind, block] for kind in range(3)], axis=1)
                    for block in (first, second)
                ],
                axis=0,
            )
            projected += dot(jnp.concatenate([left, right], axis=1), both)
        rounded = projected.astype(BF16)
        k_nat[rows, :] = rounded[:, 128:256]
        values = rounded[:, 256:384]
        lane = lax.broadcasted_iota(jnp.int32, values.shape, 1)
        v_diag[rows, :] = jnp.where(lane < DH, values, jnp.zeros_like(values))
        v_diag[pl.ds(T + 128 * chunk, 128), :] = jnp.where(lane >= DH, values, jnp.zeros_like(values))
        turned = rounded.astype(F32).T
        q_t[:, rows] = turned[0:128].astype(BF16)
        k_t[:, rows] = turned[128:256]
        v_t[:, rows] = turned[256:384].astype(BF16)
    right = v_diag[...]
    for (shift, first), (_, second) in zip(feature_rows(k_t[0:DH, :]), feature_rows(k_t[DH:, :])):
        state = dot(jnp.concatenate([first, second], axis=1), right).astype(BF16)
        if shift == SHIFTS:
            for y in range(PLANE):
                sent[y, MAIN : MAIN + EDGE, :] = state[EDGE * y : EDGE * (y + 1)]
        else:
            y, start = divmod(DH * shift, MAIN)
            sent[y, start : start + DH, :] = state
    gram = dot(k_t[...].astype(BF16), k_nat[...])
    lane = lax.broadcasted_iota(jnp.int32, (DH, 128), 1)
    gram = jnp.where(lane < DH, gram[0:DH], gram[DH:]).astype(BF16)
    for y in range(PLANE):
        sent[y, MAIN + EDGE :, :] = gram[EDGE * y : EDGE * (y + 1)]


def merge_kernel(blocks, total):
    def summed(start, size):
        rows = slice(start, start + size)
        parts = [blocks[y, rows, :].astype(F32) for y in range(PLANE)]
        while len(parts) > 1:
            parts = [a + b for a, b in zip(parts[::2], parts[1::2])]
        return parts[0]

    for z in range(PLANES):
        total[z, 0:32, :] = summed(32 * z, 32).astype(BF16)
    last, gram = summed(MAIN, EDGE), summed(MAIN + EDGE, EDGE)
    row = lax.broadcasted_iota(jnp.int32, (PLANES, 8, 128), 1)
    extra = jnp.where(row == 0, last[:, None, :], jnp.where(row == 1, gram[:, None, :], 0.0))
    total[:, 32:40, :] = extra.astype(BF16)


def prefix_kernel(blocks, prefix):
    running = jnp.zeros((PIECE, 128), F32)
    for z in range(PLANES):
        prefix[z] = running.astype(BF16)
        if z < PLANES - 1:
            running += blocks[z].astype(F32)


def spread_kernel(prefix, blocks, out):
    def spread(running, start, size):
        rows = slice(start, start + size)
        for y in range(PLANE):
            out[y, rows, :] = running.astype(BF16)
            if y < PLANE - 1:
                running += blocks[y, rows, :].astype(F32)

    for z in range(PLANES):
        spread(prefix[z, 0:32, :].astype(F32), 32 * z, 32)
    extra = prefix[:, 32:40, :].astype(F32)
    spread(extra[:, 0, :], MAIN, EDGE)
    spread(extra[:, 1, :], MAIN + EDGE, EDGE)


def local_kernel(q_t, k_nat, v_t, gain, num, den, column):
    column[...] = jnp.broadcast_to(gain[...].astype(F32), (128, 128)).T
    queries = q_t[...]
    row = lax.broadcasted_iota(jnp.int32, queries.shape, 0)
    for h in range(2):
        masked = jnp.where((row >= DH * h) & (row < DH * (h + 1)), queries, jnp.zeros_like(queries))
        for j in range(2):
            cols = slice(256 * j, 256 * (j + 1))
            total = jnp.zeros((DH, 256), F32)
            weight_sum = jnp.zeros((1, 256), F32)
            for i in range(j + 1):
                scores = dot(k_nat[256 * i : 256 * (i + 1), :], masked[:, cols])
                weights = scores * scores * (1.0 / DH)
                if i == j:
                    s_ids = lax.broadcasted_iota(jnp.int32, weights.shape, 0)
                    t_ids = lax.broadcasted_iota(jnp.int32, weights.shape, 1)
                    weights = jnp.where(s_ids <= t_ids, weights, 0.0)
                weight_sum += jnp.sum(weights, axis=0, keepdims=True)
                values = v_t[DH * h : DH * (h + 1), 256 * i : 256 * (i + 1)]
                total += dot(values, weights.astype(BF16))
            num[DH * h : DH * (h + 1), cols] = total
            den[h : h + 1, cols] = weight_sum
    den[2:8, :] = jnp.zeros((6, T), F32)


def finish_kernel(core, prefix, num, den, q_t, gain, weights, keep, give, feats):
    c = core[0]
    gram = jnp.concatenate([prefix[y, MAIN + EDGE :, :] for y in range(PLANE)], axis=0).astype(F32).T
    gram = gram.astype(BF16)
    dens = []
    for h in range(2):
        queries = q_t[DH * h : DH * (h + 1), :]
        wide = queries.astype(F32)
        both = dot(gram[DH * h : DH * (h + 1), :], queries)
        dens.append(jnp.sum(both * wide, axis=0, keepdims=True) * (1.0 / DH))
        for shift, product in feature_rows(wide):
            scale = (1.0 if shift in (0, SHIFTS) else 2.0) / DH
            feats[h, DH * shift : DH * (shift + 1), :] = product * jnp.asarray(scale, BF16)
    sums = [num[0:DH, :], num[DH:, :]]
    for group in range(9):
        if group < 8:
            y, start = divmod(256 * group, MAIN)
            state = prefix[y, start : start + 256, :]
        else:
            state = jnp.concatenate([prefix[y, MAIN : MAIN + EDGE, :] for y in range(PLANE)], axis=0)
        turned = state.astype(F32).T.astype(BF16)
        rows = pl.ds(256 * group, 256 if group < 8 else DH)
        for h in range(2):
            sums[h] += dot(turned[DH * h : DH * (h + 1), :], feats[h, rows, :])
    attended = jnp.concatenate(
        [sums[h] / (1.0 + den[h : h + 1, :] + dens[h]) for h in range(2)], axis=0
    )
    squares = jnp.sum(attended * attended, axis=0, keepdims=True)
    column = gain[...]
    mixed = jnp.concatenate(
        [attended[:, 128 * i : 128 * (i + 1)] * column for i in range(4)], axis=1
    ).astype(BF16)
    extra = split_rows(squares)
    for x in range(4):
        keep[x, 0:128, :] = dot(weights[2 * x + c], mixed).astype(BF16)
        give[x, 0:128, :] = dot(weights[2 * x + 1 - c], mixed).astype(BF16)
        keep[x, 128:136, :] = extra
        give[x, 128:136, :] = extra


def split_rows(squares):
    high = squares.astype(BF16).astype(F32)
    row = lax.broadcasted_iota(jnp.int32, (8, T), 0)
    return jnp.where(row == 0, high, jnp.where(row == 1, squares - high, 0.0)).astype(BF16)


def pair_kernel(keep, received, out):
    for x in range(4):
        out[x, 0:128, :] = (keep[x, 0:128, :].astype(F32) + received[x, 0:128, :].astype(F32)).astype(BF16)
        extra = keep[x, 128:136, :].astype(F32) + received[x, 128:136, :].astype(F32)
        out[x, 128:136, :] = split_rows(jnp.sum(extra, axis=0, keepdims=True))


def output_kernel(parts, hidden, out):
    total = parts[0, 0:128, :].astype(F32)
    extra = parts[0, 128:136, :].astype(F32)
    for x in range(1, 4):
        total += parts[x, 0:128, :].astype(F32)
        extra += parts[x, 128:136, :].astype(F32)
    squares = jnp.sum(extra, axis=0, keepdims=True)
    update = total * lax.rsqrt(squares / D + EPSILON)
    out[...] = (hidden[...].astype(F32) + update.T).astype(BF16)


def exchange(blocks, axis, groups):
    return lax.all_to_all(blocks, axis, 0, 0, axis_index_groups=groups)


def shards(tokens, w_qkv, w_out, gain_in, gain_mid):
    core = (lax.axis_index("head") & 1).astype(jnp.int32)[None]
    shape = jax.ShapeDtypeStruct
    weights = w_qkv[0].transpose(1, 0, 2).reshape(3, 8, 128, 128)
    gains = gain_in.reshape(8, 128).astype(F32)
    out_weights = w_out[0].reshape(128, 8, 128).transpose(1, 2, 0)
    own = exchange(jnp.broadcast_to(tokens, (4, T, 128)), "head", X_GROUPS)
    other = lax.ppermute(own, "head", CORE_SWAP)
    sent, q_t, k_nat, v_t = call(
        project_kernel,
        (
            shape((PLANE, SLICE, 128), BF16),
            shape((128, T), BF16),
            shape((T, 128), BF16),
            shape((128, T), BF16),
        ),
        scratch=[pltpu.VMEM((128, T), F32), pltpu.VMEM((2 * T, 128), BF16)],
        flops=2 * T * D * 384 + 2 * 2112 * T * 256,
        moved=3000000,
        in_specs=[SMEM, VMEM, VMEM, VMEM, VMEM],
        out_specs=(VMEM,) * 4,
    )(core, own, other, gains, weights)
    blocks = exchange(sent, "seq", NEAR_GROUPS)
    num, den, gain = call(
        local_kernel,
        (shape((128, T), F32), shape((8, T), F32), shape((128, 128), F32)),
        flops=2 * 2 * T * T * 128,
        moved=1000000,
        in_specs=[VMEM] * 4,
        out_specs=(VMEM,) * 3,
    )(q_t, k_nat, v_t, gain_mid)
    pieces = shape((PLANES, PIECE, 128), BF16)
    total = call(merge_kernel, pieces, moved=800000, in_specs=[VMEM], out_specs=VMEM)(blocks)
    received = exchange(total, "seq", FAR_GROUPS)
    prefix = call(prefix_kernel, pieces, moved=400000, in_specs=[VMEM], out_specs=VMEM)(received)
    prefix = exchange(prefix, "seq", FAR_GROUPS)
    spread = call(
        spread_kernel,
        shape((PLANE, SLICE, 128), BF16),
        moved=1300000,
        in_specs=[VMEM] * 2,
        out_specs=VMEM,
    )(prefix, blocks)
    spread = exchange(spread, "seq", NEAR_GROUPS)
    partial = shape((4, 136, T), BF16)
    keep, give = call(
        finish_kernel,
        (partial, partial),
        scratch=[pltpu.VMEM((2, 2112, T), BF16)],
        flops=2 * 2112 * T * 128,
        moved=2500000,
        in_specs=[SMEM] + [VMEM] * 6,
        out_specs=(VMEM,) * 2,
    )(core, spread, num, den, q_t, gain, out_weights)
    received = lax.ppermute(give, "head", CORE_SWAP)
    paired = call(pair_kernel, partial, moved=1600000, in_specs=[VMEM] * 2, out_specs=VMEM)(
        keep, received
    )
    parts = exchange(paired, "head", X_GROUPS)
    return call(
        output_kernel,
        shape((T, 128), BF16),
        moved=900000,
        in_specs=[VMEM] * 2,
        out_specs=VMEM,
    )(parts, tokens)


def solution(mesh):
    placed = (
        P("seq", "head"),
        P(None, None, None, "head"),
        P(None, "head", None),
        P(),
        P(None, "head"),
    )
    return jax.shard_map(
        shards, mesh=mesh, in_specs=placed, out_specs=P("seq", "head"), check_vma=False
    )
```

```python
import jax
import jax.numpy as jnp
from jax import lax
from jax.experimental import pallas as pl
from jax.experimental.pallas import tpu as pltpu
from jax.sharding import PartitionSpec as P

D = 1024
H = 16
DH = 64
T = 512
EPSILON = 1e-06
SHIFTS = 32
PLANE = 16
PLANES = 4
MAIN = 2048 // PLANE
EDGE = DH // PLANE
SLICE = MAIN + 2 * EDGE
F32 = jnp.float32
BF16 = jnp.bfloat16
VMEM = pl.BlockSpec(memory_space=pltpu.VMEM)
SMEM = pl.BlockSpec(memory_space=pltpu.SMEM)
X_GROUPS = [[0, 2, 4, 6], [1, 3, 5, 7]]
NEAR_GROUPS = [[PLANE * z + y for y in range(PLANE)] for z in range(PLANES)]
FAR_GROUPS = [[PLANE * z + y for z in range(PLANES)] for y in range(PLANE)]
CORE_SWAP = [(h, h ^ 1) for h in range(8)]


def dot(a, b):
    return jnp.dot(a, b, preferred_element_type=F32)


def call(kernel, outs, scratch=(), flops=0, moved=0, **kw):
    return pl.pallas_call(
        kernel,
        out_shape=outs,
        scratch_shapes=list(scratch),
        cost_estimate=pl.CostEstimate(flops=flops, bytes_accessed=moved, transcendentals=0),
        compiler_params=pltpu.CompilerParams(vmem_limit_bytes=40 * 1024 * 1024),
        **kw,
    )


def feature_rows(wide):
    base = wide.astype(BF16)
    for low in range(16):
        turned = (pltpu.roll(wide, DH - low, 0) if low else wide).astype(BF16)
        for high in range(3):
            shift = 16 * high + low
            if shift > SHIFTS:
                continue
            moved = turned
            if high:
                moved = jnp.concatenate([turned[16 * high :], turned[: 16 * high]], axis=0)
            yield shift, base * moved


def project_kernel(core, own, other, gain, weights, sent, q_t, k_nat, v_t, k_t, v_diag):
    c = core[0]
    for chunk in range(4):
        rows = pl.ds(128 * chunk, 128)
        total = jnp.zeros((128, 1), F32)
        for x in range(4):
            for part in (own, other):
                wide = part[x, rows, :].astype(F32)
                total += jnp.sum(wide * wide, axis=1, keepdims=True)
        inverse = lax.rsqrt(total / D + EPSILON)
        projected = jnp.zeros((128, 384), F32)
        for x in range(4):
            first, second = 2 * x + c, 2 * x + 1 - c
            left = (own[x, rows, :].astype(F32) * inverse * gain[pl.ds(first, 1), :]).astype(BF16)
            right = (other[x, rows, :].astype(F32) * inverse * gain[pl.ds(second, 1), :]).astype(BF16)
            both = jnp.concatenate(
                [
                    jnp.concatenate([weights[kind, block] for kind in range(3)], axis=1)
                    for block in (first, second)
                ],
                axis=0,
            )
            projected += dot(jnp.concatenate([left, right], axis=1), both)
        rounded = projected.astype(BF16)
        k_nat[rows, :] = rounded[:, 128:256]
        values = rounded[:, 256:384]
        lane = lax.broadcasted_iota(jnp.int32, values.shape, 1)
        v_diag[rows, :] = jnp.where(lane < DH, values, jnp.zeros_like(values))
        v_diag[pl.ds(T + 128 * chunk, 128), :] = jnp.where(lane >= DH, values, jnp.zeros_like(values))
        turned = rounded.astype(F32).T
        q_t[:, rows] = turned[0:128].astype(BF16)
        k_t[:, rows] = turned[128:256]
        v_t[:, rows] = turned[256:384].astype(BF16)
    right = v_diag[...]
    last = None
    for (shift, first), (_, second) in zip(feature_rows(k_t[0:DH, :]), feature_rows(k_t[DH:, :])):
        state = dot(jnp.concatenate([first, second], axis=1), right).astype(BF16)
        if shift == SHIFTS:
            last = state
        else:
            y, start = divmod(DH * shift, MAIN)
            sent[y, start : start + DH, :] = state
    gram = dot(k_t[...].astype(BF16), k_nat[...])
    lane = lax.broadcasted_iota(jnp.int32, (DH, 128), 1)
    gram = jnp.where(lane < DH, gram[0:DH], gram[DH:]).astype(BF16)
    edge = dot(edge_rows(128, DH, 0), last) + dot(edge_rows(128, DH, EDGE), gram)
    sent[:, MAIN:, :] = edge.astype(BF16).reshape(PLANE, 2 * EDGE, 128)


def edge_rows(rows, columns, offset):
    row = lax.broadcasted_iota(jnp.int32, (rows, columns), 0)
    column = lax.broadcasted_iota(jnp.int32, (rows, columns), 1)
    place, a = (row, column) if rows == 128 else (column, row)
    hit = place == 2 * EDGE * (a // EDGE) + a % EDGE + offset
    return jnp.where(hit, 1.0, 0.0).astype(BF16)


def merge_kernel(blocks, total):
    parts = [blocks[y].astype(F32) for y in range(PLANE)]
    while len(parts) > 1:
        parts = [a + b for a, b in zip(parts[::2], parts[1::2])]
    total[...] = parts[0].astype(BF16)


def spread_kernel(first, second, third, fourth, blocks, out):
    running = (first[...].astype(F32) + second[...].astype(F32)) + (
        third[...].astype(F32) + fourth[...].astype(F32)
    )
    for y in range(PLANE):
        out[y] = running.astype(BF16)
        if y < PLANE - 1:
            running += blocks[y].astype(F32)


def local_kernel(q_t, k_nat, v_t, gain, num, den, column):
    column[...] = jnp.broadcast_to(gain[...].astype(F32), (128, 128)).T
    queries = q_t[...]
    row = lax.broadcasted_iota(jnp.int32, queries.shape, 0)
    for h in range(2):
        masked = jnp.where((row >= DH * h) & (row < DH * (h + 1)), queries, jnp.zeros_like(queries))
        for j in range(2):
            cols = slice(256 * j, 256 * (j + 1))
            total = jnp.zeros((DH, 256), F32)
            weight_sum = jnp.zeros((1, 256), F32)
            for i in range(j + 1):
                scores = dot(k_nat[256 * i : 256 * (i + 1), :], masked[:, cols])
                weights = scores * scores * (1.0 / DH)
                if i == j:
                    s_ids = lax.broadcasted_iota(jnp.int32, weights.shape, 0)
                    t_ids = lax.broadcasted_iota(jnp.int32, weights.shape, 1)
                    weights = jnp.where(s_ids <= t_ids, weights, 0.0)
                weight_sum += jnp.sum(weights, axis=0, keepdims=True)
                values = v_t[DH * h : DH * (h + 1), 256 * i : 256 * (i + 1)]
                total += dot(values, weights.astype(BF16))
            num[DH * h : DH * (h + 1), cols] = total
            den[h : h + 1, cols] = weight_sum
    den[2:8, :] = jnp.zeros((6, T), F32)


def finish_kernel(core, prefix, num, den, q_t, gain, weights, keep, give, feats):
    c = core[0]
    edge = prefix[:, MAIN:, :].reshape(128, 128)
    gram = dot(edge_rows(DH, 128, EDGE), edge).T.astype(BF16)
    dens = []
    for h in range(2):
        queries = q_t[DH * h : DH * (h + 1), :]
        wide = queries.astype(F32)
        both = dot(gram[DH * h : DH * (h + 1), :], queries)
        dens.append(jnp.sum(both * wide, axis=0, keepdims=True) * (1.0 / DH))
        for shift, product in feature_rows(wide):
            scale = (1.0 if shift in (0, SHIFTS) else 2.0) / DH
            feats[h, DH * shift : DH * (shift + 1), :] = product * jnp.asarray(scale, BF16)
    sums = [num[0:DH, :], num[DH:, :]]
    for group in range(9):
        if group < 8:
            state = jnp.concatenate([prefix[2 * group, 0:MAIN, :], prefix[2 * group + 1, 0:MAIN, :]], axis=0)
        else:
            state = dot(edge_rows(DH, 128, 0), edge)
        turned = state.astype(F32).T.astype(BF16)
        rows = pl.ds(256 * group, 256 if group < 8 else DH)
        for h in range(2):
            sums[h] += dot(turned[DH * h : DH * (h + 1), :], feats[h, rows, :])
    attended = jnp.concatenate(
        [sums[h] / (1.0 + den[h : h + 1, :] + dens[h]) for h in range(2)], axis=0
    )
    squares = jnp.sum(attended * attended, axis=0, keepdims=True)
    column = gain[...]
    mixed = jnp.concatenate(
        [attended[:, 128 * i : 128 * (i + 1)] * column for i in range(4)], axis=1
    ).astype(BF16)
    extra = split_rows(squares)
    for x in range(4):
        keep[x, 0:128, :] = dot(weights[2 * x + c], mixed).astype(BF16)
        give[x, 0:128, :] = dot(weights[2 * x + 1 - c], mixed).astype(BF16)
        keep[x, 128:136, :] = extra
        give[x, 128:136, :] = extra


def split_rows(squares):
    high = squares.astype(BF16).astype(F32)
    row = lax.broadcasted_iota(jnp.int32, (8, T), 0)
    return jnp.where(row == 0, high, jnp.where(row == 1, squares - high, 0.0)).astype(BF16)


def pair_kernel(keep, received, out):
    for x in range(4):
        out[x, 0:128, :] = (keep[x, 0:128, :].astype(F32) + received[x, 0:128, :].astype(F32)).astype(BF16)
        extra = keep[x, 128:136, :].astype(F32) + received[x, 128:136, :].astype(F32)
        out[x, 128:136, :] = split_rows(jnp.sum(extra, axis=0, keepdims=True))


def output_kernel(parts, hidden, out):
    total = parts[0, 0:128, :].astype(F32)
    extra = parts[0, 128:136, :].astype(F32)
    for x in range(1, 4):
        total += parts[x, 0:128, :].astype(F32)
        extra += parts[x, 128:136, :].astype(F32)
    squares = jnp.sum(extra, axis=0, keepdims=True)
    update = total * lax.rsqrt(squares / D + EPSILON)
    out[...] = (hidden[...].astype(F32) + update.T).astype(BF16)


def exchange(blocks, axis, groups):
    return lax.all_to_all(blocks, axis, 0, 0, axis_index_groups=groups)


def forward(total, pairs):
    return lax.ppermute(
        total, "seq", [(PLANE * a + i, PLANE * b + i) for a, b in pairs for i in range(PLANE)]
    )


def shards(tokens, w_qkv, w_out, gain_in, gain_mid):
    core = (lax.axis_index("head") & 1).astype(jnp.int32)[None]
    shape = jax.ShapeDtypeStruct
    weights = w_qkv[0].transpose(1, 0, 2).reshape(3, 8, 128, 128)
    gains = gain_in.reshape(8, 128).astype(F32)
    out_weights = w_out[0].reshape(128, 8, 128).transpose(1, 2, 0)
    own = exchange(jnp.broadcast_to(tokens, (4, T, 128)), "head", X_GROUPS)
    other = lax.ppermute(own, "head", CORE_SWAP)
    sent, q_t, k_nat, v_t = call(
        project_kernel,
        (
            shape((PLANE, SLICE, 128), BF16),
            shape((128, T), BF16),
            shape((T, 128), BF16),
            shape((128, T), BF16),
        ),
        scratch=[pltpu.VMEM((128, T), F32), pltpu.VMEM((2 * T, 128), BF16)],
        flops=2 * T * D * 384 + 2 * 2112 * T * 256,
        moved=3000000,
        in_specs=[SMEM, VMEM, VMEM, VMEM, VMEM],
        out_specs=(VMEM,) * 4,
    )(core, own, other, gains, weights)
    blocks = exchange(sent, "seq", NEAR_GROUPS)
    num, den, gain = call(
        local_kernel,
        (shape((128, T), F32), shape((8, T), F32), shape((128, 128), F32)),
        flops=2 * 2 * T * T * 128,
        moved=1000000,
        in_specs=[VMEM] * 4,
        out_specs=(VMEM,) * 3,
    )(q_t, k_nat, v_t, gain_mid)
    total = call(
        merge_kernel,
        shape((SLICE, 128), BF16),
        moved=800000,
        in_specs=[VMEM],
        out_specs=VMEM,
    )(blocks)
    direct = forward(total, ((0, 1), (2, 3)))
    earlier = [direct, forward(total, ((0, 3),)), forward(total, ((1, 3),))]
    earlier.append(forward(total + direct, ((1, 2),)))
    spread = call(
        spread_kernel,
        shape((PLANE, SLICE, 128), BF16),
        moved=1300000,
        in_specs=[VMEM] * 5,
        out_specs=VMEM,
    )(*earlier, blocks)
    spread = exchange(spread, "seq", NEAR_GROUPS)
    partial = shape((4, 136, T), BF16)
    keep, give = call(
        finish_kernel,
        (partial, partial),
        scratch=[pltpu.VMEM((2, 2112, T), BF16)],
        flops=2 * 2112 * T * 128,
        moved=2500000,
        in_specs=[SMEM] + [VMEM] * 6,
        out_specs=(VMEM,) * 2,
    )(core, spread, num, den, q_t, gain, out_weights)
    received = lax.ppermute(give, "head", CORE_SWAP)
    paired = call(pair_kernel, partial, moved=1600000, in_specs=[VMEM] * 2, out_specs=VMEM)(
        keep, received
    )
    parts = exchange(paired, "head", X_GROUPS)
    return call(
        output_kernel,
        shape((T, 128), BF16),
        moved=900000,
        in_specs=[VMEM] * 2,
        out_specs=VMEM,
    )(parts, tokens)


def solution(mesh):
    placed = (
        P("seq", "head"),
        P(None, None, None, "head"),
        P(None, "head", None),
        P(),
        P(None, "head"),
    )
    return jax.shard_map(
        shards, mesh=mesh, in_specs=placed, out_specs=P("seq", "head"), check_vma=False
    )
```

```python
import jax
import jax.numpy as jnp
from jax import lax
from jax.experimental import pallas as pl
from jax.experimental.pallas import tpu as pltpu
from jax.sharding import PartitionSpec as P

D = 1024
H = 16
DH = 64
T = 512
EPSILON = 1e-06
SHIFTS = 32
PLANE = 8
PLANES = 8
WIDE = 2 * PLANE
MAIN = 2048 // PLANE
EDGE = DH // PLANE
SLICE = MAIN + 2 * EDGE
F32 = jnp.float32
BF16 = jnp.bfloat16
VMEM = pl.BlockSpec(memory_space=pltpu.VMEM)
SMEM = pl.BlockSpec(memory_space=pltpu.SMEM)
X_GROUPS = [[0, 2, 4, 6], [1, 3, 5, 7]]
NEAR_GROUPS = [[PLANE * z + y for y in range(PLANE)] for z in range(PLANES)]
PAIR_SWAP = [(b, b ^ PLANE) for b in range(PLANE * PLANES)]
CORE_SWAP = [(h, h ^ 1) for h in range(8)]


def dot(a, b):
    return jnp.dot(a, b, preferred_element_type=F32)


def call(kernel, outs, scratch=(), flops=0, moved=0, **kw):
    return pl.pallas_call(
        kernel,
        out_shape=outs,
        scratch_shapes=list(scratch),
        cost_estimate=pl.CostEstimate(flops=flops, bytes_accessed=moved, transcendentals=0),
        compiler_params=pltpu.CompilerParams(vmem_limit_bytes=40 * 1024 * 1024),
        **kw,
    )


def feature_rows(wide):
    base = wide.astype(BF16)
    for low in range(16):
        turned = (pltpu.roll(wide, DH - low, 0) if low else wide).astype(BF16)
        for high in range(3):
            shift = 16 * high + low
            if shift > SHIFTS:
                continue
            moved = turned
            if high:
                moved = jnp.concatenate([turned[16 * high :], turned[: 16 * high]], axis=0)
            yield shift, base * moved


def project_kernel(core, own, other, gain, weights, sent, q_t, k_nat, v_t, k_t, v_diag):
    c = core[0]
    for chunk in range(4):
        rows = pl.ds(128 * chunk, 128)
        total = jnp.zeros((128, 1), F32)
        for x in range(4):
            for part in (own, other):
                wide = part[x, rows, :].astype(F32)
                total += jnp.sum(wide * wide, axis=1, keepdims=True)
        inverse = lax.rsqrt(total / D + EPSILON)
        projected = jnp.zeros((128, 384), F32)
        for x in range(4):
            first, second = 2 * x + c, 2 * x + 1 - c
            left = (own[x, rows, :].astype(F32) * inverse * gain[pl.ds(first, 1), :]).astype(BF16)
            right = (other[x, rows, :].astype(F32) * inverse * gain[pl.ds(second, 1), :]).astype(BF16)
            both = jnp.concatenate(
                [
                    jnp.concatenate([weights[kind, block] for kind in range(3)], axis=1)
                    for block in (first, second)
                ],
                axis=0,
            )
            projected += dot(jnp.concatenate([left, right], axis=1), both)
        rounded = projected.astype(BF16)
        k_nat[rows, :] = rounded[:, 128:256]
        values = rounded[:, 256:384]
        lane = lax.broadcasted_iota(jnp.int32, values.shape, 1)
        v_diag[rows, :] = jnp.where(lane < DH, values, jnp.zeros_like(values))
        v_diag[pl.ds(T + 128 * chunk, 128), :] = jnp.where(lane >= DH, values, jnp.zeros_like(values))
        turned = rounded.astype(F32).T
        q_t[:, rows] = turned[0:128].astype(BF16)
        k_t[:, rows] = turned[128:256]
        v_t[:, rows] = turned[256:384].astype(BF16)
    right = v_diag[...]
    for (shift, first), (_, second) in zip(feature_rows(k_t[0:DH, :]), feature_rows(k_t[DH:, :])):
        state = dot(jnp.concatenate([first, second], axis=1), right).astype(BF16)
        if shift == SHIFTS:
            for y in range(PLANE):
                sent[y, MAIN : MAIN + EDGE, :] = state[EDGE * y : EDGE * (y + 1)]
        else:
            y, start = divmod(DH * shift, MAIN)
            sent[y, start : start + DH, :] = state
    gram = dot(k_t[...].astype(BF16), k_nat[...])
    lane = lax.broadcasted_iota(jnp.int32, (DH, 128), 1)
    gram = jnp.where(lane < DH, gram[0:DH], gram[DH:]).astype(BF16)
    for y in range(PLANE):
        sent[y, MAIN + EDGE :, :] = gram[EDGE * y : EDGE * (y + 1)]


def merge_kernel(blocks, total):
    parts = [blocks[y].astype(F32) for y in range(PLANE)]
    while len(parts) > 1:
        parts = [a + b for a, b in zip(parts[::2], parts[1::2])]
    total[...] = parts[0].astype(BF16)


def spread_kernel(odd, partner, first, second, third, fourth, blocks, out):
    running = (first[...].astype(F32) + second[...].astype(F32)) + (
        third[...].astype(F32) + fourth[...].astype(F32)
    )
    running += jnp.where(odd[0] == 1, partner[...].astype(F32), 0.0)
    for y in range(PLANE):
        out[y] = running.astype(BF16)
        if y < PLANE - 1:
            running += blocks[y].astype(F32)


def local_kernel(q_t, k_nat, v_t, gain, num, den, column):
    column[...] = jnp.broadcast_to(gain[...].astype(F32), (128, 128)).T
    queries = q_t[...]
    row = lax.broadcasted_iota(jnp.int32, queries.shape, 0)
    for h in range(2):
        masked = jnp.where((row >= DH * h) & (row < DH * (h + 1)), queries, jnp.zeros_like(queries))
        for j in range(2):
            cols = slice(256 * j, 256 * (j + 1))
            total = jnp.zeros((DH, 256), F32)
            weight_sum = jnp.zeros((1, 256), F32)
            for i in range(j + 1):
                scores = dot(k_nat[256 * i : 256 * (i + 1), :], masked[:, cols])
                weights = scores * scores * (1.0 / DH)
                if i == j:
                    s_ids = lax.broadcasted_iota(jnp.int32, weights.shape, 0)
                    t_ids = lax.broadcasted_iota(jnp.int32, weights.shape, 1)
                    weights = jnp.where(s_ids <= t_ids, weights, 0.0)
                weight_sum += jnp.sum(weights, axis=0, keepdims=True)
                values = v_t[DH * h : DH * (h + 1), 256 * i : 256 * (i + 1)]
                total += dot(values, weights.astype(BF16))
            num[DH * h : DH * (h + 1), cols] = total
            den[h : h + 1, cols] = weight_sum
    den[2:8, :] = jnp.zeros((6, T), F32)


def finish_kernel(core, prefix, num, den, q_t, gain, weights, keep, give, feats):
    c = core[0]
    gram = jnp.concatenate([prefix[y, MAIN + EDGE :, :] for y in range(PLANE)], axis=0).astype(F32).T
    gram = gram.astype(BF16)
    dens = []
    for h in range(2):
        queries = q_t[DH * h : DH * (h + 1), :]
        wide = queries.astype(F32)
        both = dot(gram[DH * h : DH * (h + 1), :], queries)
        dens.append(jnp.sum(both * wide, axis=0, keepdims=True) * (1.0 / DH))
        for shift, product in feature_rows(wide):
            scale = (1.0 if shift in (0, SHIFTS) else 2.0) / DH
            feats[h, DH * shift : DH * (shift + 1), :] = product * jnp.asarray(scale, BF16)
    sums = [num[0:DH, :], num[DH:, :]]
    for group in range(9):
        if group < 8:
            y, start = divmod(256 * group, MAIN)
            state = prefix[y, start : start + 256, :]
        else:
            state = jnp.concatenate([prefix[y, MAIN : MAIN + EDGE, :] for y in range(PLANE)], axis=0)
        turned = state.astype(F32).T.astype(BF16)
        rows = pl.ds(256 * group, 256 if group < 8 else DH)
        for h in range(2):
            sums[h] += dot(turned[DH * h : DH * (h + 1), :], feats[h, rows, :])
    attended = jnp.concatenate(
        [sums[h] / (1.0 + den[h : h + 1, :] + dens[h]) for h in range(2)], axis=0
    )
    squares = jnp.sum(attended * attended, axis=0, keepdims=True)
    column = gain[...]
    mixed = jnp.concatenate(
        [attended[:, 128 * i : 128 * (i + 1)] * column for i in range(4)], axis=1
    ).astype(BF16)
    extra = split_rows(squares)
    for x in range(4):
        keep[x, 0:128, :] = dot(weights[2 * x + c], mixed).astype(BF16)
        give[x, 0:128, :] = dot(weights[2 * x + 1 - c], mixed).astype(BF16)
        keep[x, 128:136, :] = extra
        give[x, 128:136, :] = extra


def split_rows(squares):
    high = squares.astype(BF16).astype(F32)
    row = lax.broadcasted_iota(jnp.int32, (8, T), 0)
    return jnp.where(row == 0, high, jnp.where(row == 1, squares - high, 0.0)).astype(BF16)


def pair_kernel(keep, received, out):
    for x in range(4):
        out[x, 0:128, :] = (keep[x, 0:128, :].astype(F32) + received[x, 0:128, :].astype(F32)).astype(BF16)
        extra = keep[x, 128:136, :].astype(F32) + received[x, 128:136, :].astype(F32)
        out[x, 128:136, :] = split_rows(jnp.sum(extra, axis=0, keepdims=True))


def output_kernel(parts, hidden, out):
    total = parts[0, 0:128, :].astype(F32)
    extra = parts[0, 128:136, :].astype(F32)
    for x in range(1, 4):
        total += parts[x, 0:128, :].astype(F32)
        extra += parts[x, 128:136, :].astype(F32)
    squares = jnp.sum(extra, axis=0, keepdims=True)
    update = total * lax.rsqrt(squares / D + EPSILON)
    out[...] = (hidden[...].astype(F32) + update.T).astype(BF16)


def exchange(blocks, axis, groups):
    return lax.all_to_all(blocks, axis, 0, 0, axis_index_groups=groups)


def forward(total, pairs):
    return lax.ppermute(
        total, "seq", [(WIDE * a + i, WIDE * b + i) for a, b in pairs for i in range(WIDE)]
    )


def shards(tokens, w_qkv, w_out, gain_in, gain_mid):
    core = (lax.axis_index("head") & 1).astype(jnp.int32)[None]
    shape = jax.ShapeDtypeStruct
    weights = w_qkv[0].transpose(1, 0, 2).reshape(3, 8, 128, 128)
    gains = gain_in.reshape(8, 128).astype(F32)
    out_weights = w_out[0].reshape(128, 8, 128).transpose(1, 2, 0)
    own = exchange(jnp.broadcast_to(tokens, (4, T, 128)), "head", X_GROUPS)
    other = lax.ppermute(own, "head", CORE_SWAP)
    sent, q_t, k_nat, v_t = call(
        project_kernel,
        (
            shape((PLANE, SLICE, 128), BF16),
            shape((128, T), BF16),
            shape((T, 128), BF16),
            shape((128, T), BF16),
        ),
        scratch=[pltpu.VMEM((128, T), F32), pltpu.VMEM((2 * T, 128), BF16)],
        flops=2 * T * D * 384 + 2 * 2112 * T * 256,
        moved=3000000,
        in_specs=[SMEM, VMEM, VMEM, VMEM, VMEM],
        out_specs=(VMEM,) * 4,
    )(core, own, other, gains, weights)
    blocks = exchange(sent, "seq", NEAR_GROUPS)
    num, den, gain = call(
        local_kernel,
        (shape((128, T), F32), shape((8, T), F32), shape((128, 128), F32)),
        flops=2 * 2 * T * T * 128,
        moved=1000000,
        in_specs=[VMEM] * 4,
        out_specs=(VMEM,) * 3,
    )(q_t, k_nat, v_t, gain_mid)
    total = call(
        merge_kernel,
        shape((SLICE, 128), BF16),
        moved=800000,
        in_specs=[VMEM],
        out_specs=VMEM,
    )(blocks)
    partner = lax.ppermute(total, "seq", PAIR_SWAP)
    total = total + partner
    direct = forward(total, ((0, 1), (2, 3)))
    earlier = [direct, forward(total, ((1, 3),)), forward(total, ((0, 3),))]
    earlier.append(forward(total + direct, ((1, 2),)))
    odd = ((lax.axis_index("seq") // PLANE) & 1).astype(jnp.int32)[None]
    spread = call(
        spread_kernel,
        shape((PLANE, SLICE, 128), BF16),
        moved=1300000,
        in_specs=[SMEM] + [VMEM] * 6,
        out_specs=VMEM,
    )(odd, partner, *earlier, blocks)
    spread = exchange(spread, "seq", NEAR_GROUPS)
    partial = shape((4, 136, T), BF16)
    keep, give = call(
        finish_kernel,
        (partial, partial),
        scratch=[pltpu.VMEM((2, 2112, T), BF16)],
        flops=2 * 2112 * T * 128,
        moved=2500000,
        in_specs=[SMEM] + [VMEM] * 6,
        out_specs=(VMEM,) * 2,
    )(core, spread, num, den, q_t, gain, out_weights)
    received = lax.ppermute(give, "head", CORE_SWAP)
    paired = call(pair_kernel, partial, moved=1600000, in_specs=[VMEM] * 2, out_specs=VMEM)(
        keep, received
    )
    parts = exchange(paired, "head", X_GROUPS)
    return call(
        output_kernel,
        shape((T, 128), BF16),
        moved=900000,
        in_specs=[VMEM] * 2,
        out_specs=VMEM,
    )(parts, tokens)


def solution(mesh):
    placed = (
        P("seq", "head"),
        P(None, None, None, "head"),
        P(None, "head", None),
        P(),
        P(None, "head"),
    )
    return jax.shard_map(
        shards, mesh=mesh, in_specs=placed, out_specs=P("seq", "head"), check_vma=False
    )
```

```python
import jax
import jax.numpy as jnp
from jax import lax
from jax.experimental import pallas as pl
from jax.experimental.pallas import tpu as pltpu
from jax.sharding import PartitionSpec as P

D = 1024
H = 16
DH = 64
T = 512
EPSILON = 1e-06
SHIFTS = 32
PLANE = 8
PLANES = 8
WIDE = 2 * PLANE
MAIN = 2048 // PLANE
EDGE = DH // PLANE
SLICE = MAIN + 2 * EDGE
F32 = jnp.float32
BF16 = jnp.bfloat16
VMEM = pl.BlockSpec(memory_space=pltpu.VMEM)
SMEM = pl.BlockSpec(memory_space=pltpu.SMEM)
X_GROUPS = [[0, 2, 4, 6], [1, 3, 5, 7]]
NEAR_GROUPS = [[PLANE * z + y for y in range(PLANE)] for z in range(PLANES)]
PAIR_SWAP = [(b, b ^ PLANE) for b in range(PLANE * PLANES)]
CORE_SWAP = [(h, h ^ 1) for h in range(8)]


def dot(a, b):
    return jnp.dot(a, b, preferred_element_type=F32)


def call(kernel, outs, scratch=(), flops=0, moved=0, **kw):
    return pl.pallas_call(
        kernel,
        out_shape=outs,
        scratch_shapes=list(scratch),
        cost_estimate=pl.CostEstimate(flops=flops, bytes_accessed=moved, transcendentals=0),
        compiler_params=pltpu.CompilerParams(vmem_limit_bytes=40 * 1024 * 1024),
        **kw,
    )


def feature_rows(wide):
    base = wide.astype(BF16)
    for low in range(16):
        turned = (pltpu.roll(wide, DH - low, 0) if low else wide).astype(BF16)
        for high in range(3):
            shift = 16 * high + low
            if shift > SHIFTS:
                continue
            moved = turned
            if high:
                moved = jnp.concatenate([turned[16 * high :], turned[: 16 * high]], axis=0)
            yield shift, base * moved


def project_kernel(core, own, other, gain, weights, sent, q_t, k_nat, v_t, k_t, v_diag):
    c = core[0]
    for chunk in range(4):
        rows = pl.ds(128 * chunk, 128)
        total = jnp.zeros((128, 1), F32)
        for x in range(4):
            for part in (own, other):
                wide = part[x, rows, :].astype(F32)
                total += jnp.sum(wide * wide, axis=1, keepdims=True)
        inverse = lax.rsqrt(total / D + EPSILON)
        projected = jnp.zeros((128, 384), F32)
        for x in range(4):
            first, second = 2 * x + c, 2 * x + 1 - c
            left = (own[x, rows, :].astype(F32) * inverse * gain[pl.ds(first, 1), :]).astype(BF16)
            right = (other[x, rows, :].astype(F32) * inverse * gain[pl.ds(second, 1), :]).astype(BF16)
            both = jnp.concatenate(
                [
                    jnp.concatenate([weights[kind, block] for kind in range(3)], axis=1)
                    for block in (first, second)
                ],
                axis=0,
            )
            projected += dot(jnp.concatenate([left, right], axis=1), both)
        rounded = projected.astype(BF16)
        k_nat[rows, :] = rounded[:, 128:256]
        values = rounded[:, 256:384]
        lane = lax.broadcasted_iota(jnp.int32, values.shape, 1)
        v_diag[rows, :] = jnp.where(lane < DH, values, jnp.zeros_like(values))
        v_diag[pl.ds(T + 128 * chunk, 128), :] = jnp.where(lane >= DH, values, jnp.zeros_like(values))
        turned = rounded.astype(F32).T
        q_t[:, rows] = turned[0:128].astype(BF16)
        k_t[:, rows] = turned[128:256]
        v_t[:, rows] = turned[256:384].astype(BF16)
    right = v_diag[...]
    for (shift, first), (_, second) in zip(feature_rows(k_t[0:DH, :]), feature_rows(k_t[DH:, :])):
        state = dot(jnp.concatenate([first, second], axis=1), right).astype(BF16)
        if shift == SHIFTS:
            for y in range(PLANE):
                sent[y, MAIN : MAIN + EDGE, :] = state[EDGE * y : EDGE * (y + 1)]
        else:
            y, start = divmod(DH * shift, MAIN)
            sent[y, start : start + DH, :] = state
    gram = dot(k_t[...].astype(BF16), k_nat[...])
    lane = lax.broadcasted_iota(jnp.int32, (DH, 128), 1)
    gram = jnp.where(lane < DH, gram[0:DH], gram[DH:]).astype(BF16)
    for y in range(PLANE):
        sent[y, MAIN + EDGE :, :] = gram[EDGE * y : EDGE * (y + 1)]


def merge_kernel(blocks, total):
    parts = [blocks[y].astype(F32) for y in range(PLANE)]
    while len(parts) > 1:
        parts = [a + b for a, b in zip(parts[::2], parts[1::2])]
    total[...] = parts[0].astype(BF16)


def spread_kernel(odd, group, partner, swapped, second, third, blocks, out):
    running = second[...].astype(F32) + third[...].astype(F32)
    running += jnp.where(group[0] > 0, swapped[...].astype(F32), 0.0)
    running += jnp.where(odd[0] == 1, partner[...].astype(F32), 0.0)
    for y in range(PLANE):
        out[y] = running.astype(BF16)
        if y < PLANE - 1:
            running += blocks[y].astype(F32)


def local_kernel(q_t, k_nat, v_t, gain, num, den, column):
    column[...] = jnp.broadcast_to(gain[...].astype(F32), (128, 128)).T
    queries = q_t[...]
    row = lax.broadcasted_iota(jnp.int32, queries.shape, 0)
    for h in range(2):
        masked = jnp.where((row >= DH * h) & (row < DH * (h + 1)), queries, jnp.zeros_like(queries))
        for j in range(2):
            cols = slice(256 * j, 256 * (j + 1))
            total = jnp.zeros((DH, 256), F32)
            weight_sum = jnp.zeros((1, 256), F32)
            for i in range(j + 1):
                scores = dot(k_nat[256 * i : 256 * (i + 1), :], masked[:, cols])
                weights = scores * scores * (1.0 / DH)
                if i == j:
                    s_ids = lax.broadcasted_iota(jnp.int32, weights.shape, 0)
                    t_ids = lax.broadcasted_iota(jnp.int32, weights.shape, 1)
                    weights = jnp.where(s_ids <= t_ids, weights, 0.0)
                weight_sum += jnp.sum(weights, axis=0, keepdims=True)
                values = v_t[DH * h : DH * (h + 1), 256 * i : 256 * (i + 1)]
                total += dot(values, weights.astype(BF16))
            num[DH * h : DH * (h + 1), cols] = total
            den[h : h + 1, cols] = weight_sum
    den[2:8, :] = jnp.zeros((6, T), F32)


def finish_kernel(core, prefix, num, den, q_t, gain, weights, keep, give, feats):
    c = core[0]
    gram = jnp.concatenate([prefix[y, MAIN + EDGE :, :] for y in range(PLANE)], axis=0).astype(F32).T
    gram = gram.astype(BF16)
    dens = []
    for h in range(2):
        queries = q_t[DH * h : DH * (h + 1), :]
        wide = queries.astype(F32)
        both = dot(gram[DH * h : DH * (h + 1), :], queries)
        dens.append(jnp.sum(both * wide, axis=0, keepdims=True) * (1.0 / DH))
        for shift, product in feature_rows(wide):
            scale = (1.0 if shift in (0, SHIFTS) else 2.0) / DH
            feats[h, DH * shift : DH * (shift + 1), :] = product * jnp.asarray(scale, BF16)
    sums = [num[0:DH, :], num[DH:, :]]
    for group in range(9):
        if group < 8:
            y, start = divmod(256 * group, MAIN)
            state = prefix[y, start : start + 256, :]
        else:
            state = jnp.concatenate([prefix[y, MAIN : MAIN + EDGE, :] for y in range(PLANE)], axis=0)
        turned = state.astype(F32).T.astype(BF16)
        rows = pl.ds(256 * group, 256 if group < 8 else DH)
        for h in range(2):
            sums[h] += dot(turned[DH * h : DH * (h + 1), :], feats[h, rows, :])
    attended = jnp.concatenate(
        [sums[h] / (1.0 + den[h : h + 1, :] + dens[h]) for h in range(2)], axis=0
    )
    squares = jnp.sum(attended * attended, axis=0, keepdims=True)
    column = gain[...]
    mixed = jnp.concatenate(
        [attended[:, 128 * i : 128 * (i + 1)] * column for i in range(4)], axis=1
    ).astype(BF16)
    extra = split_rows(squares)
    for x in range(4):
        keep[x, 0:128, :] = dot(weights[2 * x + c], mixed).astype(BF16)
        give[x, 0:128, :] = dot(weights[2 * x + 1 - c], mixed).astype(BF16)
        keep[x, 128:136, :] = extra
        give[x, 128:136, :] = extra


def split_rows(squares):
    high = squares.astype(BF16).astype(F32)
    row = lax.broadcasted_iota(jnp.int32, (8, T), 0)
    return jnp.where(row == 0, high, jnp.where(row == 1, squares - high, 0.0)).astype(BF16)


def pair_kernel(keep, received, out):
    for x in range(4):
        out[x, 0:128, :] = (keep[x, 0:128, :].astype(F32) + received[x, 0:128, :].astype(F32)).astype(BF16)
        extra = keep[x, 128:136, :].astype(F32) + received[x, 128:136, :].astype(F32)
        out[x, 128:136, :] = split_rows(jnp.sum(extra, axis=0, keepdims=True))


def output_kernel(parts, hidden, out):
    total = parts[0, 0:128, :].astype(F32)
    extra = parts[0, 128:136, :].astype(F32)
    for x in range(1, 4):
        total += parts[x, 0:128, :].astype(F32)
        extra += parts[x, 128:136, :].astype(F32)
    squares = jnp.sum(extra, axis=0, keepdims=True)
    update = total * lax.rsqrt(squares / D + EPSILON)
    out[...] = (hidden[...].astype(F32) + update.T).astype(BF16)


def exchange(blocks, axis, groups):
    return lax.all_to_all(blocks, axis, 0, 0, axis_index_groups=groups)


def forward(total, pairs):
    return lax.ppermute(
        total, "seq", [(WIDE * a + i, WIDE * b + i) for a, b in pairs for i in range(WIDE)]
    )


def shards(tokens, w_qkv, w_out, gain_in, gain_mid):
    core = (lax.axis_index("head") & 1).astype(jnp.int32)[None]
    shape = jax.ShapeDtypeStruct
    weights = w_qkv[0].transpose(1, 0, 2).reshape(3, 8, 128, 128)
    gains = gain_in.reshape(8, 128).astype(F32)
    out_weights = w_out[0].reshape(128, 8, 128).transpose(1, 2, 0)
    own = exchange(jnp.broadcast_to(tokens, (4, T, 128)), "head", X_GROUPS)
    other = lax.ppermute(own, "head", CORE_SWAP)
    sent, q_t, k_nat, v_t = call(
        project_kernel,
        (
            shape((PLANE, SLICE, 128), BF16),
            shape((128, T), BF16),
            shape((T, 128), BF16),
            shape((128, T), BF16),
        ),
        scratch=[pltpu.VMEM((128, T), F32), pltpu.VMEM((2 * T, 128), BF16)],
        flops=2 * T * D * 384 + 2 * 2112 * T * 256,
        moved=3000000,
        in_specs=[SMEM, VMEM, VMEM, VMEM, VMEM],
        out_specs=(VMEM,) * 4,
    )(core, own, other, gains, weights)
    blocks = exchange(sent, "seq", NEAR_GROUPS)
    num, den, gain = call(
        local_kernel,
        (shape((128, T), F32), shape((8, T), F32), shape((128, 128), F32)),
        flops=2 * 2 * T * T * 128,
        moved=1000000,
        in_specs=[VMEM] * 4,
        out_specs=(VMEM,) * 3,
    )(q_t, k_nat, v_t, gain_mid)
    total = call(
        merge_kernel,
        shape((SLICE, 128), BF16),
        moved=800000,
        in_specs=[VMEM],
        out_specs=VMEM,
    )(blocks)
    partner = lax.ppermute(total, "seq", PAIR_SWAP)
    total = total + partner
    swapped = forward(total, ((0, 1), (1, 0)))
    earlier = [swapped, forward(total, ((2, 3),)), forward(total + swapped, ((1, 2), (0, 3)))]
    place = lax.axis_index("seq")
    odd = ((place // PLANE) & 1).astype(jnp.int32)[None]
    group = (place // WIDE).astype(jnp.int32)[None]
    spread = call(
        spread_kernel,
        shape((PLANE, SLICE, 128), BF16),
        moved=1300000,
        in_specs=[SMEM] * 2 + [VMEM] * 5,
        out_specs=VMEM,
    )(odd, group, partner, *earlier, blocks)
    spread = exchange(spread, "seq", NEAR_GROUPS)
    partial = shape((4, 136, T), BF16)
    keep, give = call(
        finish_kernel,
        (partial, partial),
        scratch=[pltpu.VMEM((2, 2112, T), BF16)],
        flops=2 * 2112 * T * 128,
        moved=2500000,
        in_specs=[SMEM] + [VMEM] * 6,
        out_specs=(VMEM,) * 2,
    )(core, spread, num, den, q_t, gain, out_weights)
    received = lax.ppermute(give, "head", CORE_SWAP)
    paired = call(pair_kernel, partial, moved=1600000, in_specs=[VMEM] * 2, out_specs=VMEM)(
        keep, received
    )
    parts = exchange(paired, "head", X_GROUPS)
    return call(
        output_kernel,
        shape((T, 128), BF16),
        moved=900000,
        in_specs=[VMEM] * 2,
        out_specs=VMEM,
    )(parts, tokens)


def solution(mesh):
    placed = (
        P("seq", "head"),
        P(None, None, None, "head"),
        P(None, "head", None),
        P(),
        P(None, "head"),
    )
    return jax.shard_map(
        shards, mesh=mesh, in_specs=placed, out_specs=P("seq", "head"), check_vma=False
    )
```

```python
import jax
import jax.numpy as jnp
from jax import lax
from jax.experimental import pallas as pl
from jax.experimental.pallas import tpu as pltpu
from jax.sharding import PartitionSpec as P

D = 1024
H = 16
DH = 64
T = 512
EPSILON = 1e-06
SHIFTS = 32
PLANE = 8
PLANES = 8
WIDE = 2 * PLANE
MAIN = 2048 // PLANE
EDGE = DH // PLANE
SLICE = MAIN + 2 * EDGE
F32 = jnp.float32
BF16 = jnp.bfloat16
VMEM = pl.BlockSpec(memory_space=pltpu.VMEM)
SMEM = pl.BlockSpec(memory_space=pltpu.SMEM)
X_GROUPS = [[0, 2, 4, 6], [1, 3, 5, 7]]
NEAR_GROUPS = [[PLANE * z + y for y in range(PLANE)] for z in range(PLANES)]
PAIR_SWAP = [(b, b ^ PLANE) for b in range(PLANE * PLANES)]
CORE_SWAP = [(h, h ^ 1) for h in range(8)]


def dot(a, b):
    return jnp.dot(a, b, preferred_element_type=F32)


def call(kernel, outs, scratch=(), flops=0, moved=0, **kw):
    return pl.pallas_call(
        kernel,
        out_shape=outs,
        scratch_shapes=list(scratch),
        cost_estimate=pl.CostEstimate(flops=flops, bytes_accessed=moved, transcendentals=0),
        compiler_params=pltpu.CompilerParams(vmem_limit_bytes=40 * 1024 * 1024),
        **kw,
    )


def feature_rows(wide):
    base = wide.astype(BF16)
    for low in range(16):
        turned = (pltpu.roll(wide, DH - low, 0) if low else wide).astype(BF16)
        for high in range(3):
            shift = 16 * high + low
            if shift > SHIFTS:
                continue
            moved = turned
            if high:
                moved = jnp.concatenate([turned[16 * high :], turned[: 16 * high]], axis=0)
            yield shift, base * moved


def half_projection(part, rows, gain, weights, offset):
    squares = jnp.zeros((128, 1), F32)
    projected = jnp.zeros((128, 384), F32)
    for x in (0, 2):
        scaled, blocks = [], []
        for block in (x, x + 1):
            wide = part[block, rows, :].astype(F32)
            squares += jnp.sum(wide * wide, axis=1, keepdims=True)
            place = 2 * block + offset
            scaled.append((wide * gain[pl.ds(place, 1), :]).astype(BF16))
            blocks.append(jnp.concatenate([weights[kind, place] for kind in range(3)], axis=1))
        projected += dot(jnp.concatenate(scaled, axis=1), jnp.concatenate(blocks, axis=0))
    return squares, projected


def own_kernel(core, own, gain, weights, squares, projected):
    for chunk in range(4):
        rows = pl.ds(128 * chunk, 128)
        total, result = half_projection(own, rows, gain, weights, core[0])
        squares[rows, :] = jnp.broadcast_to(total, (128, 128))
        projected[rows, :] = result


def project_kernel(
    core, squares, partial, other, gain, weights, sent, q_t, k_nat, v_t, k_t, v_diag
):
    for chunk in range(4):
        rows = pl.ds(128 * chunk, 128)
        total, result = half_projection(other, rows, gain, weights, 1 - core[0])
        inverse = lax.rsqrt((total + squares[rows, 0:1]) / D + EPSILON)
        projected = (partial[rows, :] + result) * inverse
        rounded = projected.astype(BF16)
        k_nat[rows, :] = rounded[:, 128:256]
        values = rounded[:, 256:384]
        lane = lax.broadcasted_iota(jnp.int32, values.shape, 1)
        v_diag[rows, :] = jnp.where(lane < DH, values, jnp.zeros_like(values))
        v_diag[pl.ds(T + 128 * chunk, 128), :] = jnp.where(lane >= DH, values, jnp.zeros_like(values))
        turned = rounded.astype(F32).T
        q_t[:, rows] = turned[0:128].astype(BF16)
        k_t[:, rows] = turned[128:256]
        v_t[:, rows] = turned[256:384].astype(BF16)
    right = v_diag[...]
    for (shift, first), (_, second) in zip(feature_rows(k_t[0:DH, :]), feature_rows(k_t[DH:, :])):
        state = dot(jnp.concatenate([first, second], axis=1), right).astype(BF16)
        if shift == SHIFTS:
            for y in range(PLANE):
                sent[y, MAIN : MAIN + EDGE, :] = state[EDGE * y : EDGE * (y + 1)]
        else:
            y, start = divmod(DH * shift, MAIN)
            sent[y, start : start + DH, :] = state
    gram = dot(k_t[...].astype(BF16), k_nat[...])
    lane = lax.broadcasted_iota(jnp.int32, (DH, 128), 1)
    gram = jnp.where(lane < DH, gram[0:DH], gram[DH:]).astype(BF16)
    for y in range(PLANE):
        sent[y, MAIN + EDGE :, :] = gram[EDGE * y : EDGE * (y + 1)]


def merge_kernel(blocks, total):
    parts = [blocks[y].astype(F32) for y in range(PLANE)]
    while len(parts) > 1:
        parts = [a + b for a, b in zip(parts[::2], parts[1::2])]
    total[...] = parts[0].astype(BF16)


def spread_kernel(odd, group, partner, swapped, second, third, blocks, out):
    running = second[...].astype(F32) + third[...].astype(F32)
    running += jnp.where(group[0] > 0, swapped[...].astype(F32), 0.0)
    running += jnp.where(odd[0] == 1, partner[...].astype(F32), 0.0)
    for y in range(PLANE):
        out[y] = running.astype(BF16)
        if y < PLANE - 1:
            running += blocks[y].astype(F32)


def local_kernel(q_t, k_nat, v_t, gain, num, den, column):
    column[...] = jnp.broadcast_to(gain[...].astype(F32), (128, 128)).T
    queries = q_t[...]
    row = lax.broadcasted_iota(jnp.int32, queries.shape, 0)
    for h in range(2):
        masked = jnp.where((row >= DH * h) & (row < DH * (h + 1)), queries, jnp.zeros_like(queries))
        for j in range(2):
            cols = slice(256 * j, 256 * (j + 1))
            total = jnp.zeros((DH, 256), F32)
            weight_sum = jnp.zeros((1, 256), F32)
            for i in range(j + 1):
                scores = dot(k_nat[256 * i : 256 * (i + 1), :], masked[:, cols])
                weights = scores * scores * (1.0 / DH)
                if i == j:
                    s_ids = lax.broadcasted_iota(jnp.int32, weights.shape, 0)
                    t_ids = lax.broadcasted_iota(jnp.int32, weights.shape, 1)
                    weights = jnp.where(s_ids <= t_ids, weights, 0.0)
                weight_sum += jnp.sum(weights, axis=0, keepdims=True)
                values = v_t[DH * h : DH * (h + 1), 256 * i : 256 * (i + 1)]
                total += dot(values, weights.astype(BF16))
            num[DH * h : DH * (h + 1), cols] = total
            den[h : h + 1, cols] = weight_sum
    den[2:8, :] = jnp.zeros((6, T), F32)


def finish_kernel(core, prefix, num, den, q_t, gain, weights, keep, give, feats):
    c = core[0]
    gram = jnp.concatenate([prefix[y, MAIN + EDGE :, :] for y in range(PLANE)], axis=0).astype(F32).T
    gram = gram.astype(BF16)
    dens = []
    for h in range(2):
        queries = q_t[DH * h : DH * (h + 1), :]
        wide = queries.astype(F32)
        both = dot(gram[DH * h : DH * (h + 1), :], queries)
        dens.append(jnp.sum(both * wide, axis=0, keepdims=True) * (1.0 / DH))
        for shift, product in feature_rows(wide):
            scale = (1.0 if shift in (0, SHIFTS) else 2.0) / DH
            feats[h, DH * shift : DH * (shift + 1), :] = product * jnp.asarray(scale, BF16)
    sums = [num[0:DH, :], num[DH:, :]]
    for group in range(9):
        if group < 8:
            y, start = divmod(256 * group, MAIN)
            state = prefix[y, start : start + 256, :]
        else:
            state = jnp.concatenate([prefix[y, MAIN : MAIN + EDGE, :] for y in range(PLANE)], axis=0)
        turned = state.astype(F32).T.astype(BF16)
        rows = pl.ds(256 * group, 256 if group < 8 else DH)
        for h in range(2):
            sums[h] += dot(turned[DH * h : DH * (h + 1), :], feats[h, rows, :])
    attended = jnp.concatenate(
        [sums[h] / (1.0 + den[h : h + 1, :] + dens[h]) for h in range(2)], axis=0
    )
    squares = jnp.sum(attended * attended, axis=0, keepdims=True)
    column = gain[...]
    mixed = jnp.concatenate(
        [attended[:, 128 * i : 128 * (i + 1)] * column for i in range(4)], axis=1
    ).astype(BF16)
    extra = split_rows(squares)
    for x in range(4):
        keep[x, 0:128, :] = dot(weights[2 * x + c], mixed).astype(BF16)
        give[x, 0:128, :] = dot(weights[2 * x + 1 - c], mixed).astype(BF16)
        keep[x, 128:136, :] = extra
        give[x, 128:136, :] = extra


def split_rows(squares):
    high = squares.astype(BF16).astype(F32)
    row = lax.broadcasted_iota(jnp.int32, (8, T), 0)
    return jnp.where(row == 0, high, jnp.where(row == 1, squares - high, 0.0)).astype(BF16)


def pair_kernel(keep, received, out):
    for x in range(4):
        out[x, 0:128, :] = (keep[x, 0:128, :].astype(F32) + received[x, 0:128, :].astype(F32)).astype(BF16)
        extra = keep[x, 128:136, :].astype(F32) + received[x, 128:136, :].astype(F32)
        out[x, 128:136, :] = split_rows(jnp.sum(extra, axis=0, keepdims=True))


def output_kernel(parts, hidden, out):
    total = parts[0, 0:128, :].astype(F32)
    extra = parts[0, 128:136, :].astype(F32)
    for x in range(1, 4):
        total += parts[x, 0:128, :].astype(F32)
        extra += parts[x, 128:136, :].astype(F32)
    squares = jnp.sum(extra, axis=0, keepdims=True)
    update = total * lax.rsqrt(squares / D + EPSILON)
    out[...] = (hidden[...].astype(F32) + update.T).astype(BF16)


def exchange(blocks, axis, groups):
    return lax.all_to_all(blocks, axis, 0, 0, axis_index_groups=groups)


def forward(total, pairs):
    return lax.ppermute(
        total, "seq", [(WIDE * a + i, WIDE * b + i) for a, b in pairs for i in range(WIDE)]
    )


def shards(tokens, w_qkv, w_out, gain_in, gain_mid):
    core = (lax.axis_index("head") & 1).astype(jnp.int32)[None]
    shape = jax.ShapeDtypeStruct
    weights = w_qkv[0].transpose(1, 0, 2).reshape(3, 8, 128, 128)
    gains = gain_in.reshape(8, 128).astype(F32)
    out_weights = w_out[0].reshape(128, 8, 128).transpose(1, 2, 0)
    own = exchange(jnp.broadcast_to(tokens, (4, T, 128)), "head", X_GROUPS)
    other = lax.ppermute(own, "head", CORE_SWAP)
    squares, projected = call(
        own_kernel,
        (shape((T, 128), F32), shape((T, 384), F32)),
        flops=T * D * 384,
        moved=2500000,
        in_specs=[SMEM] + [VMEM] * 3,
        out_specs=(VMEM,) * 2,
    )(core, own, gains, weights)
    sent, q_t, k_nat, v_t = call(
        project_kernel,
        (
            shape((PLANE, SLICE, 128), BF16),
            shape((128, T), BF16),
            shape((T, 128), BF16),
            shape((128, T), BF16),
        ),
        scratch=[pltpu.VMEM((128, T), F32), pltpu.VMEM((2 * T, 128), BF16)],
        flops=2 * T * D * 384 + 2 * 2112 * T * 256,
        moved=3000000,
        in_specs=[SMEM] + [VMEM] * 5,
        out_specs=(VMEM,) * 4,
    )(core, squares, projected, other, gains, weights)
    blocks = exchange(sent, "seq", NEAR_GROUPS)
    num, den, gain = call(
        local_kernel,
        (shape((128, T), F32), shape((8, T), F32), shape((128, 128), F32)),
        flops=2 * 2 * T * T * 128,
        moved=1000000,
        in_specs=[VMEM] * 4,
        out_specs=(VMEM,) * 3,
    )(q_t, k_nat, v_t, gain_mid)
    total = call(
        merge_kernel,
        shape((SLICE, 128), BF16),
        moved=800000,
        in_specs=[VMEM],
        out_specs=VMEM,
    )(blocks)
    partner = lax.ppermute(total, "seq", PAIR_SWAP)
    total = total + partner
    swapped = forward(total, ((0, 1), (1, 0)))
    earlier = [swapped, forward(total, ((2, 3),)), forward(total + swapped, ((1, 2), (0, 3)))]
    place = lax.axis_index("seq")
    odd = ((place // PLANE) & 1).astype(jnp.int32)[None]
    group = (place // WIDE).astype(jnp.int32)[None]
    spread = call(
        spread_kernel,
        shape((PLANE, SLICE, 128), BF16),
        moved=1300000,
        in_specs=[SMEM] * 2 + [VMEM] * 5,
        out_specs=VMEM,
    )(odd, group, partner, *earlier, blocks)
    spread = exchange(spread, "seq", NEAR_GROUPS)
    partial = shape((4, 136, T), BF16)
    keep, give = call(
        finish_kernel,
        (partial, partial),
        scratch=[pltpu.VMEM((2, 2112, T), BF16)],
        flops=2 * 2112 * T * 128,
        moved=2500000,
        in_specs=[SMEM] + [VMEM] * 6,
        out_specs=(VMEM,) * 2,
    )(core, spread, num, den, q_t, gain, out_weights)
    received = lax.ppermute(give, "head", CORE_SWAP)
    paired = call(pair_kernel, partial, moved=1600000, in_specs=[VMEM] * 2, out_specs=VMEM)(
        keep, received
    )
    parts = exchange(paired, "head", X_GROUPS)
    return call(
        output_kernel,
        shape((T, 128), BF16),
        moved=900000,
        in_specs=[VMEM] * 2,
        out_specs=VMEM,
    )(parts, tokens)


def solution(mesh):
    placed = (
        P("seq", "head"),
        P(None, None, None, "head"),
        P(None, "head", None),
        P(),
        P(None, "head"),
    )
    return jax.shard_map(
        shards, mesh=mesh, in_specs=placed, out_specs=P("seq", "head"), check_vma=False
    )
```

```python
import jax
import jax.numpy as jnp
from jax import lax
from jax.experimental import pallas as pl
from jax.experimental.pallas import tpu as pltpu
from jax.sharding import PartitionSpec as P

D = 1024
H = 16
DH = 64
T = 512
EPSILON = 1e-06
SHIFTS = 32
PLANE = 8
PLANES = 8
WIDE = 2 * PLANE
MAIN = 2048 // PLANE
EDGE = DH // PLANE
SLICE = MAIN + 2 * EDGE
F32 = jnp.float32
BF16 = jnp.bfloat16
VMEM = pl.BlockSpec(memory_space=pltpu.VMEM)
SMEM = pl.BlockSpec(memory_space=pltpu.SMEM)
X_GROUPS = [[0, 2, 4, 6], [1, 3, 5, 7]]
NEAR_GROUPS = [[PLANE * z + y for y in range(PLANE)] for z in range(PLANES)]
PAIR_SWAP = [(b, b ^ PLANE) for b in range(PLANE * PLANES)]
CORE_SWAP = [(h, h ^ 1) for h in range(8)]


def dot(a, b):
    return jnp.dot(a, b, preferred_element_type=F32)


def call(kernel, outs, scratch=(), flops=0, moved=0, **kw):
    return pl.pallas_call(
        kernel,
        out_shape=outs,
        scratch_shapes=list(scratch),
        cost_estimate=pl.CostEstimate(flops=flops, bytes_accessed=moved, transcendentals=0),
        compiler_params=pltpu.CompilerParams(vmem_limit_bytes=40 * 1024 * 1024),
        **kw,
    )


def feature_rows(wide):
    base = wide.astype(BF16)
    for low in range(16):
        turned = (pltpu.roll(wide, DH - low, 0) if low else wide).astype(BF16)
        for high in range(3):
            shift = 16 * high + low
            if shift > SHIFTS:
                continue
            moved = turned
            if high:
                moved = jnp.concatenate([turned[16 * high :], turned[: 16 * high]], axis=0)
            yield shift, base * moved


def half_projection(part, rows, gain, weights, offset):
    squares = jnp.zeros((128, 1), F32)
    projected = jnp.zeros((128, 384), F32)
    for x in (0, 2):
        scaled, blocks = [], []
        for block in (x, x + 1):
            wide = part[block, rows, :].astype(F32)
            squares += jnp.sum(wide * wide, axis=1, keepdims=True)
            place = 2 * block + offset
            scaled.append((wide * gain[pl.ds(place, 1), :]).astype(BF16))
            blocks.append(jnp.concatenate([weights[kind, place] for kind in range(3)], axis=1))
        projected += dot(jnp.concatenate(scaled, axis=1), jnp.concatenate(blocks, axis=0))
    return squares, projected


def own_kernel(core, own, gain, weights, squares, projected):
    for chunk in range(4):
        rows = pl.ds(128 * chunk, 128)
        total, result = half_projection(own, rows, gain, weights, core[0])
        squares[rows, :] = jnp.broadcast_to(total, (128, 128))
        projected[rows, :] = result


def project_kernel(
    core, squares, partial, other, gain, weights, sent, q_t, k_nat, v_t, k_t, v_diag
):
    for chunk in range(4):
        rows = pl.ds(128 * chunk, 128)
        total, result = half_projection(other, rows, gain, weights, 1 - core[0])
        inverse = lax.rsqrt((total + squares[rows, 0:1]) / D + EPSILON)
        projected = (partial[rows, :] + result) * inverse
        rounded = projected.astype(BF16)
        k_nat[rows, :] = rounded[:, 128:256]
        values = rounded[:, 256:384]
        lane = lax.broadcasted_iota(jnp.int32, values.shape, 1)
        v_diag[rows, :] = jnp.where(lane < DH, values, jnp.zeros_like(values))
        v_diag[pl.ds(T + 128 * chunk, 128), :] = jnp.where(lane >= DH, values, jnp.zeros_like(values))
        turned = rounded.astype(F32).T
        q_t[:, rows] = turned[0:128].astype(BF16)
        k_t[:, rows] = turned[128:256]
        v_t[:, rows] = turned[256:384].astype(BF16)
    right = v_diag[...]
    for (shift, first), (_, second) in zip(feature_rows(k_t[0:DH, :]), feature_rows(k_t[DH:, :])):
        state = dot(jnp.concatenate([first, second], axis=1), right).astype(BF16)
        if shift == SHIFTS:
            for y in range(PLANE):
                sent[y, MAIN : MAIN + EDGE, :] = state[EDGE * y : EDGE * (y + 1)]
        else:
            y, start = divmod(DH * shift, MAIN)
            sent[y, start : start + DH, :] = state
    gram = dot(k_t[...].astype(BF16), k_nat[...])
    lane = lax.broadcasted_iota(jnp.int32, (DH, 128), 1)
    gram = jnp.where(lane < DH, gram[0:DH], gram[DH:]).astype(BF16)
    for y in range(PLANE):
        sent[y, MAIN + EDGE :, :] = gram[EDGE * y : EDGE * (y + 1)]


def merge_kernel(blocks, total):
    parts = [blocks[y].astype(F32) for y in range(PLANE)]
    while len(parts) > 1:
        parts = [a + b for a, b in zip(parts[::2], parts[1::2])]
    total[...] = parts[0].astype(BF16)


def spread_kernel(odd, group, partner, swapped, second, third, blocks, out):
    running = second[...].astype(F32) + third[...].astype(F32)
    running += jnp.where(group[0] > 0, swapped[...].astype(F32), 0.0)
    running += jnp.where(odd[0] == 1, partner[...].astype(F32), 0.0)
    for y in range(PLANE):
        out[y] = running.astype(BF16)
        if y < PLANE - 1:
            running += blocks[y].astype(F32)


def local_kernel(q_t, k_nat, v_t, gain, num, den, column):
    column[...] = jnp.broadcast_to(gain[...].astype(F32), (128, 128)).T
    queries = q_t[...]
    row = lax.broadcasted_iota(jnp.int32, queries.shape, 0)
    for h in range(2):
        masked = jnp.where((row >= DH * h) & (row < DH * (h + 1)), queries, jnp.zeros_like(queries))
        for j in range(2):
            cols = slice(256 * j, 256 * (j + 1))
            total = jnp.zeros((DH, 256), F32)
            weight_sum = jnp.zeros((1, 256), F32)
            for i in range(j + 1):
                scores = dot(k_nat[256 * i : 256 * (i + 1), :], masked[:, cols])
                weights = scores * scores * (1.0 / DH)
                if i == j:
                    s_ids = lax.broadcasted_iota(jnp.int32, weights.shape, 0)
                    t_ids = lax.broadcasted_iota(jnp.int32, weights.shape, 1)
                    weights = jnp.where(s_ids <= t_ids, weights, 0.0)
                weight_sum += jnp.sum(weights, axis=0, keepdims=True)
                values = v_t[DH * h : DH * (h + 1), 256 * i : 256 * (i + 1)]
                total += dot(values, weights.astype(BF16))
            num[DH * h : DH * (h + 1), cols] = total
            den[h : h + 1, cols] = weight_sum
    den[2:8, :] = jnp.zeros((6, T), F32)


def finish_kernel(core, prefix, num, den, q_t, gain, weights, mixed_out, extra_out, give, feats):
    c = core[0]
    gram = jnp.concatenate([prefix[y, MAIN + EDGE :, :] for y in range(PLANE)], axis=0).astype(F32).T
    gram = gram.astype(BF16)
    dens = []
    for h in range(2):
        queries = q_t[DH * h : DH * (h + 1), :]
        wide = queries.astype(F32)
        both = dot(gram[DH * h : DH * (h + 1), :], queries)
        dens.append(jnp.sum(both * wide, axis=0, keepdims=True) * (1.0 / DH))
        for shift, product in feature_rows(wide):
            scale = (1.0 if shift in (0, SHIFTS) else 2.0) / DH
            feats[h, DH * shift : DH * (shift + 1), :] = product * jnp.asarray(scale, BF16)
    sums = [num[0:DH, :], num[DH:, :]]
    for group in range(9):
        if group < 8:
            y, start = divmod(256 * group, MAIN)
            state = prefix[y, start : start + 256, :]
        else:
            state = jnp.concatenate([prefix[y, MAIN : MAIN + EDGE, :] for y in range(PLANE)], axis=0)
        turned = state.astype(F32).T.astype(BF16)
        rows = pl.ds(256 * group, 256 if group < 8 else DH)
        for h in range(2):
            sums[h] += dot(turned[DH * h : DH * (h + 1), :], feats[h, rows, :])
    attended = jnp.concatenate(
        [sums[h] / (1.0 + den[h : h + 1, :] + dens[h]) for h in range(2)], axis=0
    )
    squares = jnp.sum(attended * attended, axis=0, keepdims=True)
    column = gain[...]
    mixed = jnp.concatenate(
        [attended[:, 128 * i : 128 * (i + 1)] * column for i in range(4)], axis=1
    ).astype(BF16)
    extra = split_rows(squares)
    for x in range(4):
        give[x, 0:128, :] = dot(weights[2 * x + 1 - c], mixed).astype(BF16)
        give[x, 128:136, :] = extra
    mixed_out[...] = mixed
    extra_out[...] = extra


def keep_kernel(core, mixed, extra, weights, keep):
    for x in range(4):
        keep[x, 0:128, :] = dot(weights[2 * x + core[0]], mixed[...]).astype(BF16)
        keep[x, 128:136, :] = extra[...]


def split_rows(squares):
    high = squares.astype(BF16).astype(F32)
    row = lax.broadcasted_iota(jnp.int32, (8, T), 0)
    return jnp.where(row == 0, high, jnp.where(row == 1, squares - high, 0.0)).astype(BF16)


def pair_kernel(keep, received, out):
    for x in range(4):
        out[x, 0:128, :] = (keep[x, 0:128, :].astype(F32) + received[x, 0:128, :].astype(F32)).astype(BF16)
        extra = keep[x, 128:136, :].astype(F32) + received[x, 128:136, :].astype(F32)
        out[x, 128:136, :] = split_rows(jnp.sum(extra, axis=0, keepdims=True))


def output_kernel(parts, hidden, out):
    total = parts[0, 0:128, :].astype(F32)
    extra = parts[0, 128:136, :].astype(F32)
    for x in range(1, 4):
        total += parts[x, 0:128, :].astype(F32)
        extra += parts[x, 128:136, :].astype(F32)
    squares = jnp.sum(extra, axis=0, keepdims=True)
    update = total * lax.rsqrt(squares / D + EPSILON)
    out[...] = (hidden[...].astype(F32) + update.T).astype(BF16)


def exchange(blocks, axis, groups):
    return lax.all_to_all(blocks, axis, 0, 0, axis_index_groups=groups)


def forward(total, pairs):
    return lax.ppermute(
        total, "seq", [(WIDE * a + i, WIDE * b + i) for a, b in pairs for i in range(WIDE)]
    )


def shards(tokens, w_qkv, w_out, gain_in, gain_mid):
    core = (lax.axis_index("head") & 1).astype(jnp.int32)[None]
    shape = jax.ShapeDtypeStruct
    weights = w_qkv[0].transpose(1, 0, 2).reshape(3, 8, 128, 128)
    gains = gain_in.reshape(8, 128).astype(F32)
    out_weights = w_out[0].reshape(128, 8, 128).transpose(1, 2, 0)
    own = exchange(jnp.broadcast_to(tokens, (4, T, 128)), "head", X_GROUPS)
    other = lax.ppermute(own, "head", CORE_SWAP)
    squares, projected = call(
        own_kernel,
        (shape((T, 128), F32), shape((T, 384), F32)),
        flops=T * D * 384,
        moved=2500000,
        in_specs=[SMEM] + [VMEM] * 3,
        out_specs=(VMEM,) * 2,
    )(core, own, gains, weights)
    sent, q_t, k_nat, v_t = call(
        project_kernel,
        (
            shape((PLANE, SLICE, 128), BF16),
            shape((128, T), BF16),
            shape((T, 128), BF16),
            shape((128, T), BF16),
        ),
        scratch=[pltpu.VMEM((128, T), F32), pltpu.VMEM((2 * T, 128), BF16)],
        flops=2 * T * D * 384 + 2 * 2112 * T * 256,
        moved=3000000,
        in_specs=[SMEM] + [VMEM] * 5,
        out_specs=(VMEM,) * 4,
    )(core, squares, projected, other, gains, weights)
    blocks = exchange(sent, "seq", NEAR_GROUPS)
    num, den, gain = call(
        local_kernel,
        (shape((128, T), F32), shape((8, T), F32), shape((128, 128), F32)),
        flops=2 * 2 * T * T * 128,
        moved=1000000,
        in_specs=[VMEM] * 4,
        out_specs=(VMEM,) * 3,
    )(q_t, k_nat, v_t, gain_mid)
    total = call(
        merge_kernel,
        shape((SLICE, 128), BF16),
        moved=800000,
        in_specs=[VMEM],
        out_specs=VMEM,
    )(blocks)
    partner = lax.ppermute(total, "seq", PAIR_SWAP)
    total = total + partner
    swapped = forward(total, ((0, 1), (1, 0)))
    earlier = [swapped, forward(total, ((2, 3),)), forward(total + swapped, ((1, 2), (0, 3)))]
    place = lax.axis_index("seq")
    odd = ((place // PLANE) & 1).astype(jnp.int32)[None]
    group = (place // WIDE).astype(jnp.int32)[None]
    spread = call(
        spread_kernel,
        shape((PLANE, SLICE, 128), BF16),
        moved=1300000,
        in_specs=[SMEM] * 2 + [VMEM] * 5,
        out_specs=VMEM,
    )(odd, group, partner, *earlier, blocks)
    spread = exchange(spread, "seq", NEAR_GROUPS)
    partial = shape((4, 136, T), BF16)
    mixed, extra, give = call(
        finish_kernel,
        (shape((128, T), BF16), shape((8, T), BF16), partial),
        scratch=[pltpu.VMEM((2, 2112, T), BF16)],
        flops=2 * 2112 * T * 128,
        moved=2500000,
        in_specs=[SMEM] + [VMEM] * 6,
        out_specs=(VMEM,) * 3,
    )(core, spread, num, den, q_t, gain, out_weights)
    received = lax.ppermute(give, "head", CORE_SWAP)
    keep = call(
        keep_kernel,
        partial,
        flops=T * D * 128,
        moved=900000,
        in_specs=[SMEM] + [VMEM] * 3,
        out_specs=VMEM,
    )(core, mixed, extra, out_weights)
    paired = call(pair_kernel, partial, moved=1600000, in_specs=[VMEM] * 2, out_specs=VMEM)(
        keep, received
    )
    parts = exchange(paired, "head", X_GROUPS)
    return call(
        output_kernel,
        shape((T, 128), BF16),
        moved=900000,
        in_specs=[VMEM] * 2,
        out_specs=VMEM,
    )(parts, tokens)


def solution(mesh):
    placed = (
        P("seq", "head"),
        P(None, None, None, "head"),
        P(None, "head", None),
        P(),
        P(None, "head"),
    )
    return jax.shard_map(
        shards, mesh=mesh, in_specs=placed, out_specs=P("seq", "head"), check_vma=False
    )
```
